32 devices in a mesh: blk: 8 (over y, x, core), pitch: 4 (over z).
Axes of the slice: x: 2, y: 2, z: 4, core: 2. Of those that a mesh axis runs over, the one named last changes fastest.
Arguments:
- flow_state: float32 [5, 32, 128, 128], P(None, 'pitch', 'blk'), may hold values from -0.6 to 3.2, as said below
- prior_state: float32 [5, 32, 128, 128], P(None, 'pitch', 'blk'), may hold values from -0.75 to 3.35, as said below
- fourier_store: float32 [2, 49, 10, 128, 128], P(None, None, None, ('blk', 'pitch')), may hold values from -0.15 to 2.6, as said below
- sample_times: int32 [2, 128, 128], P(None, ('blk', 'pitch')), may hold values from 0 to 95
- harmonics: int32 [128, 128], P(('blk', 'pitch')), may hold values from 12 to 24
Outputs:
- new_state: float32 [5, 32, 128, 128], P(None, 'pitch', 'blk')
- new_store: float32 [2, 49, 10, 128, 128], P(None, None, None, ('blk', 'pitch'))
- new_ghosts: float32 [2, 10, 128, 128], P(None, None, ('blk', 'pitch'))
The draws below stay inside these ranges and needn't reach their ends.
Inputs may be any that keep to these rules, and one draw needn't show every extreme that they name: `flow_state`: density between 0.7 and 1.3, momenta between -0.6 and 0.6, total energy between 2.2 and 3.2. `prior_state`: each entry within 0.15 of flow_state's. `fourier_store`: the k-th cosine and sine coefficients are at most 0.08 / k in magnitude.
All inputs are finite; a program needn't handle non-finite values.
Results may differ from the reference program's by a relative error of at most 0.000068.
Values sent between devices are 32-bit elements; how exact they have to be, the bound alone decides.
No kernel may reach another device: no remote copies, remote signals or barrier semaphores. Data moves between devices by JAX's collectives and lax.ppermute only.
A program may use at most 64 MiB of HBM per device.

```python
import math
import jax
import jax.numpy as jnp
from jax import lax

CR = 128
HARM = 24
NT = 96
NP = 32
NA = 128


def base_state(key):
    shape = (NP, NA, CR)
    keys = jax.random.split(key, 5)
    density = jax.random.uniform(keys[0], shape, jnp.float32, 0.8, 1.2)
    moments = [jax.random.uniform(keys[1 + which], shape, jnp.float32, -0.5, 0.5) for which in range(3)]
    energy = jax.random.uniform(keys[4], shape, jnp.float32, 2.3, 3.1)
    return jnp.stack([density, moments[0], moments[1], moments[2], energy])


def draw_flow_state(key, part):
    return base_state(jax.random.fold_in(key, 11))


def draw_prior_state(key, part):
    offsets = jax.random.uniform(jax.random.fold_in(key, 12), (5, NP, NA, CR), jnp.float32, -0.15, 0.15)
    return base_state(jax.random.fold_in(key, 11)) + offsets


def draw_fourier_store(key, part):
    first, second = jax.random.split(jax.random.fold_in(key, 21))
    levels = jnp.array([1.0, 1.0, 0.0, 0.0, 0.0, 0.0, 0.0, 0.0, 2.5, 2.5], jnp.float32).reshape((1, 1, 10, 1, 1))
    orders = jnp.arange(1, HARM + 1).astype(jnp.float32)
    spread = 0.1
    weights = 0.08 / jnp.concatenate([orders, orders])
    mean_part = levels + spread * jax.random.uniform(first, (2, 1, 10, NA, CR), jnp.float32, -1.0, 1.0)
    harm_part = jax.random.uniform(second, (2, 2 * HARM, 10, NA, CR), jnp.float32, -1.0, 1.0) * weights.reshape((1, 2 * HARM, 1, 1, 1))
    return jnp.concatenate([mean_part, harm_part], axis=1)


def place_ends(values, stream_key, smallest, high):
    spot = [jax.random.randint(jax.random.fold_in(stream_key, axis), (), 0, length) for axis, length in enumerate(values.shape)]
    main_axis = values.shape.index(max(values.shape))
    neighbour = spot[:main_axis] + [(spot[main_axis] + 1) % values.shape[main_axis]] + spot[main_axis + 1:]
    return values.at[tuple(spot)].set(smallest).at[tuple(neighbour)].set(high)


def setup_inputs(seed: int = 0) -> dict:
    key_list = jax.random.split(jax.random.key(seed), 6)
    return {
        "flow_state": draw_flow_state(jax.random.fold_in(key_list[5], 71), 0),
        "prior_state": draw_prior_state(jax.random.fold_in(key_list[5], 71), 0),
        "fourier_store": draw_fourier_store(jax.random.fold_in(key_list[5], 71), 0),
        "sample_times": place_ends(jax.random.randint(key_list[3], (2, NA, CR), 0, NT), jax.random.fold_in(key_list[3], 1), 0, NT - 1).astype(jnp.int32),
        "harmonics": place_ends(jax.random.randint(key_list[4], (NA, CR), HARM // 2, HARM + 1), jax.random.fold_in(key_list[4], 1), HARM // 2, HARM).astype(jnp.int32),
    }


gamma_less = 0.4
diss_coeff = 0.03125
section_coefs = (1.0 / 3.0, 0.5, 1.0)
pseudo_step = 0.1
physical_step = 0.25
relax_rate = 0.125
lag_turns = 0.3


def fluxes(current, direction):
    density = current[0]
    velocity = current[direction] / density
    pressure = gamma_less * (current[4] - 0.5 * (current[1] * current[1] + current[2] * current[2] + current[3] * current[3]) / density)
    flux_parts = [current[direction], current[1] * velocity, current[2] * velocity, current[3] * velocity, (current[4] + pressure) * velocity]
    flux_parts[direction] = flux_parts[direction] + pressure
    return jnp.stack(flux_parts)


def face_sum(padded, direction):
    cells_n = padded.shape[direction] - 4
    faces_n = cells_n + 1
    cell_flux = fluxes(padded, direction)

    def window(values, offset, length):
        return lax.slice_in_dim(values, offset, offset + length, axis=direction)

    face_flux = 0.5 * (window(cell_flux, 1, faces_n) + window(cell_flux, 2, faces_n)) - diss_coeff * (window(padded, 3, faces_n) - 3.0 * window(padded, 2, faces_n) + 3.0 * window(padded, 1, faces_n) - window(padded, 0, faces_n))
    return window(face_flux, 1, cells_n) - window(face_flux, 0, cells_n)


def harmonic_tables(phases_at, harm_count):
    orders = jnp.arange(1, harm_count + 1).astype(jnp.float32).reshape((harm_count, 1, 1))
    angles = orders * phases_at[None]
    return jnp.cos(angles), jnp.sin(angles)


def rebuild(coeffs, phases_at, active):
    harm_count = (coeffs.shape[0] - 1) // 2
    cosines, sines = harmonic_tables(phases_at, harm_count)
    orders = jnp.arange(1, harm_count + 1).astype(jnp.int32).reshape((harm_count, 1, 1))
    active_mask = (orders <= active[None]).astype(jnp.float32)
    harm_terms = coeffs[1:harm_count + 1] * (active_mask * cosines)[:, None] + coeffs[harm_count + 1:] * (active_mask * sines)[:, None]
    return coeffs[0] + jnp.sum(harm_terms, axis=0)


def refresh(coeffs, samples, phases_at):
    harm_count = (coeffs.shape[0] - 1) // 2
    cosines, sines = harmonic_tables(phases_at, harm_count)
    mean_part = (1.0 - relax_rate) * coeffs[0] + relax_rate * samples
    cos_part = (1.0 - relax_rate) * coeffs[1:harm_count + 1] + (2.0 * relax_rate) * samples[None] * cosines[:, None]
    sin_part = (1.0 - relax_rate) * coeffs[harm_count + 1:] + (2.0 * relax_rate) * samples[None] * sines[:, None]
    return jnp.concatenate([mean_part[None], cos_part, sin_part], axis=0)


def residual(current, flow_state, prior_state, low_ghost, high_ghost):
    pitch_pad = jnp.concatenate([low_ghost, current, high_ghost], axis=1)
    axial_pad = jnp.pad(current, ((0, 0), (0, 0), (2, 2), (0, 0)), mode="edge")
    radial_pad = jnp.pad(current, ((0, 0), (0, 0), (0, 0), (2, 2)), mode="edge")
    summed = face_sum(pitch_pad, 1) + face_sum(axial_pad, 2) + face_sum(radial_pad, 3)
    return summed + (3.0 * current - 4.0 * flow_state + prior_state) * (0.5 / physical_step)


def reference(flow_state, prior_state, fourier_store, sample_times, harmonics):
    period = 2.0 * math.pi / NT
    phase_lag = 2.0 * math.pi * lag_turns
    phases = sample_times.astype(jnp.float32) * period
    ghost_shape = (5, 2) + harmonics.shape
    low_ghost = rebuild(fourier_store[0], phases[0] - phase_lag, harmonics).reshape(ghost_shape)
    high_ghost = rebuild(fourier_store[1], phases[1] + phase_lag, harmonics).reshape(ghost_shape)
    current = flow_state
    for section_coef in section_coefs:
        current = flow_state - (section_coef * pseudo_step) * residual(current, flow_state, prior_state, low_ghost, high_ghost)
    next_phases = phases + period
    face_shape = (10,) + harmonics.shape
    low_store = refresh(fourier_store[0], current[:, -2:].reshape(face_shape), next_phases[0])
    high_store = refresh(fourier_store[1], current[:, :2].reshape(face_shape), next_phases[1])
    ghosts = jnp.stack([rebuild(low_store, next_phases[0] - phase_lag, harmonics), rebuild(high_store, next_phases[1] + phase_lag, harmonics)])
    return current, jnp.stack([low_store, high_store]), ghosts
```

```python
import functools
import math

import jax
import jax.numpy as jnp
from jax import lax
from jax.experimental import pallas as pl
from jax.experimental.pallas import tpu as pltpu
from jax.sharding import PartitionSpec as P

NT = 96

gamma_less = 0.4
diss_coeff = 0.03125
section_coefs = (1.0 / 3.0, 0.5, 1.0)
pseudo_step = 0.1
physical_step = 0.25
relax_rate = 0.125
lag_turns = 0.3
period = 2.0 * math.pi / NT
phase_lag = 2.0 * math.pi * lag_turns

HF = 2 * len(section_coefs)
HP = HF - 2
PAD = 8

F32 = jnp.float32
VMEM = pl.BlockSpec(memory_space=pltpu.VMEM)


def call(body, outs, *args, scratch=(), aliases=None, out_specs=None, cost=0, limit=8):
    outs = [jax.ShapeDtypeStruct(shape, F32) for shape in outs]
    moved = 4 * sum(math.prod(a.shape) for a in list(args) + outs)
    return pl.pallas_call(
        body,
        out_shape=outs,
        in_specs=[VMEM] * len(args),
        out_specs=out_specs or [VMEM] * len(outs),
        scratch_shapes=list(scratch),
        input_output_aliases=aliases or {},
        compiler_params=pltpu.CompilerParams(vmem_limit_bytes=limit << 20),
        cost_estimate=pl.CostEstimate(flops=cost, bytes_accessed=moved, transcendentals=0),
    )(*args)


def is_even(axis):
    return lax.axis_index(axis) % 2 == 0


def source_of(flow, prior):
    return (2.0 / physical_step) * flow - (0.5 / physical_step) * prior


def pack_pitch(flow_ref, prior_ref, first_ref, second_ref):
    cells = flow_ref.shape[1]
    even = is_even("pitch")
    for out_ref, top in ((first_ref, even), (second_ref, jnp.logical_not(even))):
        at = jnp.where(top, cells - HF, 0)
        out_ref[:, :HF] = flow_ref[:, pl.ds(at, HF)]
        at = jnp.where(top, cells - HP, 0)
        out_ref[:, HF:] = source_of(flow_ref[:, pl.ds(at, HP)], prior_ref[:, pl.ds(at, HP)])


def doubled(values):
    return jnp.concatenate([values, values], axis=0)


def rebuild_shares(store_ref, times_ref, active_ref, *out_refs):
    share_ref, send_refs = out_refs[0], out_refs[1:]
    harm_count = (store_ref.shape[1] - 1) // 2
    signals = store_ref.shape[2]
    active = doubled(active_ref[...])
    for which in range(2):
        angle = doubled(times_ref[which]).astype(F32) * period
        angle = angle - phase_lag if which == 0 else angle + phase_lag
        cos_1, sin_1 = jnp.cos(angle), jnp.sin(angle)
        cos_k, sin_k = cos_1, sin_1
        totals = [store_ref[which, 0, v] for v in range(signals)]
        for k in range(1, harm_count + 1):
            used = active >= k
            a, b = jnp.where(used, cos_k, 0.0), jnp.where(used, sin_k, 0.0)
            for v in range(signals):
                totals[v] = totals[v] + (
                    store_ref[which, k, v] * a + store_ref[which, harm_count + k, v] * b
                )
            cos_k, sin_k = cos_k * cos_1 - sin_k * sin_1, sin_k * cos_1 + cos_k * sin_1
        for v in range(signals):
            share_ref[which, v] = totals[v]
    at = lax.axis_index("pitch")
    for step, send_ref in enumerate(send_refs, start=1):
        send_ref[...] = share_ref[jnp.where(at == step, 0, 1)]


def prepare_close(store_ref, times_ref, active_ref, table_ref, base_ref, gain_ref):
    harm_count = (store_ref.shape[1] - 1) // 2
    signals = store_ref.shape[2]
    active = doubled(active_ref[...])
    gain = jnp.full(active.shape, relax_rate, F32)
    for k in range(1, harm_count + 1):
        gain = gain + jnp.where(active >= k, 2.0 * relax_rate * math.cos(k * phase_lag), 0.0)
    gain_ref[...] = gain
    keep = 1.0 - relax_rate
    for which in range(2):
        angle = doubled(times_ref[which]).astype(F32) * period + period
        cos_1, sin_1 = jnp.cos(angle), jnp.sin(angle)
        cos_k, sin_k = cos_1, sin_1
        totals = [store_ref[which, 0, v] for v in range(signals)]
        turn = -phase_lag if which == 0 else phase_lag
        for k in range(1, harm_count + 1):
            table_ref[which, k - 1] = (2.0 * relax_rate) * cos_k
            table_ref[which, harm_count + k - 1] = (2.0 * relax_rate) * sin_k
            used = active >= k
            c, s = math.cos(k * turn), math.sin(k * turn)
            a = jnp.where(used, cos_k * c - sin_k * s, 0.0)
            b = jnp.where(used, sin_k * c + cos_k * s, 0.0)
            for v in range(signals):
                totals[v] = totals[v] + (
                    store_ref[which, k, v] * a + store_ref[which, harm_count + k, v] * b
                )
            cos_k, sin_k = cos_k * cos_1 - sin_k * sin_1, sin_k * cos_1 + cos_k * sin_1
        for v in range(signals):
            base_ref[which, v] = keep * totals[v]


def place_own(flow_ref, prior_ref, state_ref, source_ref):
    cells, rows = flow_ref.shape[1:3]
    state_ref[:, HF : HF + cells, PAD : PAD + rows] = flow_ref[...]
    source_ref[:, HP : HP + cells, PAD : PAD + rows] = source_of(flow_ref[...], prior_ref[...])


def message_layout(variables, cells):
    parts, place = [], 0
    for v in range(variables):
        for which, width in ((0, HF), (1, HP)):
            for plane in range(1 - width, cells + width - 1):
                outside = max(0, -plane, plane - cells + 1)
                count = width - outside
                parts.append((v, which, plane + width, count, place))
                place += count
    return parts, -(-place // 8) * 8


def place_pitch(own_count, rows, *refs):
    state_in, source_in, first_ref, second_ref, share_ref = refs[:5]
    state_ref, source_ref, out_1, out_2 = refs[-4:]
    ghost_refs = refs[5:-4]
    del state_in, source_in
    cells = own_count
    even = is_even("pitch")
    own_rows = slice(PAD, PAD + rows)
    for halo_ref, upper in ((first_ref, even), (second_ref, jnp.logical_not(even))):
        at = jnp.where(upper, HF + cells, 0)
        state_ref[:, pl.ds(at, HF), own_rows] = halo_ref[:, :HF]
        at = jnp.where(upper, HP + cells, 0)
        source_ref[:, pl.ds(at, HP), own_rows] = halo_ref[:, HF:]
    slabs = len(ghost_refs) + 1
    part = rows // slabs
    pitch_at = lax.axis_index("pitch")

    def place_ghosts(plane, pieces):
        for piece, piece_rows in pieces:
            for layer in range(2):
                at = PAD + piece_rows * part
                state_ref[:, plane + layer, at : at + part] = piece[:, layer * part : (layer + 1) * part]

    @pl.when(pitch_at == 0)
    def _():
        place_ghosts(
            HF - 2,
            [(share_ref[0], 0)] + [(ghost_refs[j - 1][...], j) for j in range(1, slabs)],
        )

    @pl.when(pitch_at == slabs - 1)
    def _():
        place_ghosts(
            HF + cells,
            [(share_ref[1], slabs - 1)]
            + [(ghost_refs[j - 1][...], slabs - 1 - j) for j in range(1, slabs)],
        )

    parts, _ = message_layout(state_ref.shape[0], cells)
    blk_even = is_even("blk")

    def write(up_ref, down_ref):
        for v, which, plane, count, place in parts:
            from_ref = (state_ref, source_ref)[which]
            up_ref[place : place + count] = from_ref[v, plane, PAD + rows - count : PAD + rows]
            down_ref[place : place + count] = from_ref[v, plane, PAD : PAD + count]

    @pl.when(blk_even)
    def _():
        write(out_1, out_2)

    @pl.when(jnp.logical_not(blk_even))
    def _():
        write(out_2, out_1)


def sections(cells, rows, slabs, blocks, *refs):
    state_in, source_in, first_ref, second_ref = refs[:4]
    new_ref, own_ref = refs[4:6]
    send_refs = refs[6 : 6 + slabs - 1]
    state_ref, source_ref = refs[5 + slabs : 7 + slabs]
    mid_refs = refs[7 + slabs : 9 + slabs]
    pitch_ref, axial_ref, radial_ref = refs[9 + slabs :]
    del state_in, source_in
    variables = new_ref.shape[0]
    pitch_at = lax.axis_index("pitch")
    blk_at = lax.axis_index("blk")
    parts, _ = message_layout(variables, cells)

    def unpack(low_ref, high_ref):
        for v, which, plane, count, place in parts:
            to_ref = (state_ref, source_ref)[which]
            to_ref[v, plane, PAD - count : PAD] = low_ref[place : place + count]
            to_ref[v, plane, PAD + rows : PAD + rows + count] = high_ref[place : place + count]

    @pl.when(is_even("blk"))
    def _():
        unpack(second_ref, first_ref)

    @pl.when(jnp.logical_not(is_even("blk")))
    def _():
        unpack(first_ref, second_ref)

    def clamp_ends(ref):
        planes = ref.shape[1]

        @pl.when(blk_at == 0)
        def _():
            ref[:, :, PAD - 2 : PAD] = jnp.broadcast_to(
                ref[:, :, PAD : PAD + 1], (variables, planes, 2, ref.shape[3])
            )

        @pl.when(blk_at == blocks - 1)
        def _():
            ref[:, :, PAD + rows : PAD + rows + 2] = jnp.broadcast_to(
                ref[:, :, PAD + rows - 1 : PAD + rows], (variables, planes, 2, ref.shape[3])
            )

    def keep_ghosts(ref, width):
        @pl.when(pitch_at == 0)
        def _():
            ref[:, width - 2 : width] = state_ref[:, HF - 2 : HF]

        @pl.when(pitch_at == slabs - 1)
        def _():
            ref[:, width + cells : width + cells + 2] = state_ref[:, HF + cells : HF + cells + 2]

    clamp_ends(state_ref)
    lanes = state_ref.shape[3]

    def shift_down(values, lane):
        return jnp.where(lane == lanes - 1, values, pltpu.roll(values, lanes - 1, 1))

    def shift_up(values, lane):
        return jnp.where(lane == 0, values, pltpu.roll(values, 1, 1))

    def section(coef, from_ref, width, to_ref, out_width, row_at, count):
        def fluxes(index, carry):
            plane = index + width - out_width - 1
            u = [from_ref[v, plane] for v in range(variables)]
            inverse = 1.0 / u[0]
            speed = [u[d] * inverse for d in (1, 2, 3)]
            pressure = gamma_less * (
                u[4] - 0.5 * (u[1] * speed[0] + u[2] * speed[1] + u[3] * speed[2])
            )
            half = 0.5 * pressure
            total = u[4] + pressure
            for d, flux_ref in enumerate((pitch_ref, axial_ref, radial_ref)):
                w = 0.5 * speed[d]
                for v in (1, 2, 3):
                    flux = u[v] * w
                    flux_ref[v - 1, index] = flux + half if v == d + 1 else flux
                flux_ref[3, index] = total * w
            return carry

        planes = cells + 2 * out_width
        lax.fori_loop(0, planes + 2, fluxes, 0)
        rows_at = slice(row_at, row_at + count)

        def update(index, carry):
            plane = index + width - out_width
            lane = lax.broadcasted_iota(jnp.int32, (count, lanes), 1)
            for v in range(variables):

                def state(ahead, over):
                    return from_ref[v, plane + ahead, row_at + over : row_at + over + count]

                def flux(ref, d, ahead, over):
                    at = slice(row_at + over, row_at + over + count)
                    if v == 0:
                        return 0.5 * from_ref[d, plane + ahead, at]
                    return ref[v - 1, index + 1 + ahead, at]

                here = state(0, 0)
                change = flux(pitch_ref, 1, 1, 0) - flux(pitch_ref, 1, -1, 0)
                change = change + (flux(axial_ref, 2, 0, 1) - flux(axial_ref, 2, 0, -1))
                near = (state(1, 0) + state(-1, 0)) + (state(0, 1) + state(0, -1))
                far = (state(2, 0) + state(-2, 0)) + (state(0, 2) + state(0, -2))
                scaled = diss_coeff * here
                along = flux(radial_ref, 3, 0, 0)
                near_here = 4.0 * scaled
                ahead = shift_down(near_here + along - shift_down(scaled, lane), lane)
                behind = shift_up(near_here - along - shift_up(scaled, lane), lane)
                change = change + (ahead + behind) + diss_coeff * (4.0 * near - far)
                change = change + (1.5 / physical_step - 18.0 * diss_coeff) * here
                source = source_ref[v, index + HP - out_width, rows_at]
                flow = state_ref[v, index + HF - out_width, rows_at]
                if to_ref is new_ref:
                    to_at = slice(row_at - PAD, row_at - PAD + count)
                else:
                    to_at = rows_at
                to_ref[v, index, to_at] = flow + (coef * pseudo_step) * (source - change)
            return carry

        lax.fori_loop(0, planes, update, 0)

    last = len(section_coefs) - 1
    from_ref, width = state_ref, HF
    for step, coef in enumerate(section_coefs):
        out_width = width - 2
        if step == last:
            section(coef, from_ref, width, new_ref, 0, PAD, rows)
            break
        to_ref = mid_refs[step]
        count = -(-(rows + 2 * out_width) // 8) * 8
        section(coef, from_ref, width, to_ref, out_width, PAD - out_width, count)
        clamp_ends(to_ref)
        keep_ghosts(to_ref, out_width)
        from_ref, width = to_ref, out_width

    part = rows // slabs

    def write_face(plane, piece, out_ref):
        for layer in range(2):
            out_ref[:, layer * part : (layer + 1) * part] = new_ref[
                :, plane + layer, piece * part : (piece + 1) * part
            ]

    @pl.when(pitch_at == 0)
    def _():
        write_face(0, 0, own_ref)
        for j in range(1, slabs):
            write_face(0, j, send_refs[j - 1])

    @pl.when(pitch_at == slabs - 1)
    def _():
        write_face(cells - 2, slabs - 1, own_ref)
        for j in range(1, slabs):
            write_face(cells - 2, slabs - 1 - j, send_refs[j - 1])


def close(chunks, *refs):
    store_ref, table_ref, base_ref, gain_ref, own_ref = refs[:5]
    got_refs = refs[5:-4]
    out_ref, ghost_ref, fresh_ref, sems = refs[-4:]
    slabs = len(got_refs) + 1
    at = lax.axis_index("pitch")
    top, bottom = own_ref[...], own_ref[...]
    for j in range(1, slabs):
        got = got_refs[j - 1][...]
        top = jnp.where(at == slabs - 1 - j, got, top)
        bottom = jnp.where(at == j, got, bottom)
    keep = 1.0 - relax_rate
    count = store_ref.shape[1]
    signals = store_ref.shape[2]
    copies = []
    for which, sample in enumerate((top, bottom)):
        ghost_ref[which] = base_ref[which] + sample * gain_ref[...][None]
        for lo, hi in zip(chunks[:-1], chunks[1:]):
            for k in range(lo, hi):
                weight = relax_rate if k == 0 else table_ref[which, k - 1]
                for v in range(signals):
                    fresh_ref[which, k, v] = keep * store_ref[which, k, v] + weight * sample[v]
            copy = pltpu.make_async_copy(
                fresh_ref.at[which, pl.ds(lo, hi - lo)],
                out_ref.at[which, pl.ds(lo, hi - lo)],
                sems.at[len(copies)],
            )
            copy.start()
            copies.append(copy)
    for copy in copies:
        copy.wait()


def swap_pairs(count, start):
    pairs = [(i, i + 1) for i in range(start, count - 1, 2)]
    return pairs + [(b, a) for a, b in pairs]


def shards(flow_state, prior_state, fourier_store, sample_times, harmonics):
    slabs = lax.axis_size("pitch")
    blocks = lax.axis_size("blk")
    variables, cells, rows, lanes = flow_state.shape
    orders, signals, part = fourier_store.shape[1:4]
    store = fourier_store.reshape(2, orders, variables, 2 * part, lanes)
    halo = (variables, HF + HP, rows, lanes)
    face = (variables, 2 * part, lanes)

    first, second = call(pack_pitch, [halo, halo], flow_state, prior_state)
    first = lax.ppermute(first, "pitch", swap_pairs(slabs, 0))
    second = lax.ppermute(second, "pitch", swap_pairs(slabs, 1))

    share, *sends = call(
        rebuild_shares,
        [(2,) + face] + [face] * (slabs - 1),
        store,
        sample_times,
        harmonics,
    )
    ghosts = [
        lax.ppermute(send, "pitch", [(j, 0), (slabs - 1 - j, slabs - 1)])
        for j, send in enumerate(sends, start=1)
    ]

    long_rows = rows + 2 * PAD
    state_shape = (variables, cells + 2 * HF, long_rows, lanes)
    source_shape = (variables, cells + 2 * HP, long_rows, lanes)
    state, source = call(place_own, [state_shape, source_shape], flow_state, prior_state)
    _, length = message_layout(variables, cells)
    state, source, out_1, out_2 = call(
        functools.partial(place_pitch, cells, rows),
        [state_shape, source_shape, (length, lanes), (length, lanes)],
        state,
        source,
        first,
        second,
        share,
        *ghosts,
        aliases={0: 0, 1: 1},
    )
    got_1 = lax.ppermute(out_1, "blk", swap_pairs(blocks, 0))
    got_2 = lax.ppermute(out_2, "blk", swap_pairs(blocks, 1))
    table, base, gain = call(
        prepare_close,
        [(2, orders - 1, 2 * part, lanes), (2,) + face, (2 * part, lanes)],
        store,
        sample_times,
        harmonics,
    )
    flux_shape = (variables - 1, cells + 2 * HP + 2, long_rows, lanes)
    outs = call(
        functools.partial(sections, cells, rows, slabs, blocks),
        [flow_state.shape] + [face] * slabs + [state_shape, source_shape],
        state,
        source,
        got_1,
        got_2,
        scratch=[
            pltpu.VMEM((variables, cells + 2 * HP, long_rows, lanes), F32),
            pltpu.VMEM((variables, cells + 2 * HP - 4, long_rows, lanes), F32),
        ]
        + [pltpu.VMEM(flux_shape, F32)] * 3,
        aliases={0: 1 + slabs, 1: 2 + slabs},
        limit=16,
    )
    new_state, own, sends = outs[0], outs[1], outs[2 : 1 + slabs]
    got = [
        lax.ppermute(send, "pitch", [(0, j), (slabs - 1, slabs - 1 - j)])
        for j, send in enumerate(sends, start=1)
    ]
    pieces = 7
    chunks = [orders * i // pieces for i in range(pieces + 1)]
    new_store, new_ghosts = call(
        functools.partial(close, chunks),
        [store.shape, (2,) + face],
        store,
        table,
        base,
        gain,
        own,
        *got,
        scratch=[pltpu.VMEM(store.shape, F32), pltpu.SemaphoreType.DMA((2 * pieces,))],
        out_specs=[pl.BlockSpec(memory_space=pl.ANY), VMEM],
    )
    return (
        new_state,
        new_store.reshape(fourier_store.shape),
        new_ghosts.reshape(2, signals, part, lanes),
    )


def solution(mesh):
    placed = (
        P(None, "pitch", "blk", None),
        P(None, "pitch", "blk", None),
        P(None, None, None, ("blk", "pitch"), None),
        P(None, ("blk", "pitch"), None),
        P(("blk", "pitch"), None),
    )
    return jax.shard_map(
        shards,
        mesh=mesh,
        in_specs=placed,
        out_specs=(
            P(None, "pitch", "blk", None),
            P(None, None, None, ("blk", "pitch"), None),
            P(None, None, ("blk", "pitch"), None),
        ),
        check_vma=False,
    )
```

```python
import functools
import math

import jax
import jax.numpy as jnp
from jax import lax
from jax.experimental import pallas as pl
from jax.experimental.pallas import tpu as pltpu
from jax.sharding import PartitionSpec as P

NT = 96

gamma_less = 0.4
diss_coeff = 0.03125
section_coefs = (1.0 / 3.0, 0.5, 1.0)
pseudo_step = 0.1
physical_step = 0.25
relax_rate = 0.125
lag_turns = 0.3
period = 2.0 * math.pi / NT
phase_lag = 2.0 * math.pi * lag_turns

HF = 2 * len(section_coefs)
HP = HF - 2
PAD = 8

F32 = jnp.float32
VMEM = pl.BlockSpec(memory_space=pltpu.VMEM)


HBM = pl.BlockSpec(memory_space=pltpu.MemorySpace.HBM)


def call(body, outs, *args, scratch=(), aliases=None, in_specs=None, out_specs=None, cost=0, limit=8):
    outs = [jax.ShapeDtypeStruct(shape, F32) for shape in outs]
    moved = 4 * sum(math.prod(a.shape) for a in list(args) + outs)
    return pl.pallas_call(
        body,
        out_shape=outs,
        in_specs=in_specs or [VMEM] * len(args),
        out_specs=out_specs or [VMEM] * len(outs),
        scratch_shapes=list(scratch),
        input_output_aliases=aliases or {},
        compiler_params=pltpu.CompilerParams(vmem_limit_bytes=limit << 20),
        cost_estimate=pl.CostEstimate(flops=cost, bytes_accessed=moved, transcendentals=0),
    )(*args)


def is_even(axis):
    return lax.axis_index(axis) % 2 == 0


def source_of(flow, prior):
    return (2.0 / physical_step) * flow - (0.5 / physical_step) * prior


def start_block(flow_hbm, prior_hbm, state_ref, source_ref, first_ref, second_ref, prior_ref, sems):
    cells, rows = flow_hbm.shape[1:3]
    own_rows = slice(PAD, PAD + rows)
    flow_ref = state_ref.at[:, pl.ds(HF, cells), pl.ds(PAD, rows)]
    copies = [
        pltpu.make_async_copy(flow_hbm, flow_ref, sems.at[0]),
        pltpu.make_async_copy(prior_hbm, prior_ref, sems.at[1]),
    ]
    for copy in copies:
        copy.start()
    for copy in copies:
        copy.wait()
    even = is_even("pitch")
    source_ref[:, HP : HP + cells, own_rows] = source_of(
        state_ref[:, HF : HF + cells, own_rows], prior_ref[...]
    )
    for out_ref, top in ((first_ref, even), (second_ref, jnp.logical_not(even))):
        at = jnp.where(top, cells, HF)
        out_ref[:, :HF] = state_ref[:, pl.ds(at, HF), own_rows]
        at = jnp.where(top, cells, HP)
        out_ref[:, HF:] = source_ref[:, pl.ds(at, HP), own_rows]


def pack_axial(cells, rows, state_ref, source_ref, edge_ref, corner_ref):
    refs = (state_ref, source_ref)
    edges, _ = edge_layout(state_ref.shape[0], cells, 0)
    corners, _ = corner_layout(state_ref.shape[0])
    top = is_even("pitch")

    def write(up):
        for v, which, plane, count, place in edges:
            edge_ref[place : place + count] = refs[which][v, plane, edge_rows(rows, count, up)]
        for v, which, depth, count, place in corners:
            width = (HF, HP)[which]
            plane = jnp.where(top, width + cells - depth, width + depth - 1)
            corner_ref[place : place + count] = refs[which][v, plane, edge_rows(rows, count, up)]

    @pl.when(is_even("blk"))
    def _():
        write(False)

    @pl.when(jnp.logical_not(is_even("blk")))
    def _():
        write(True)


def edge_rows(rows, count, up):
    return slice(PAD + rows - count, PAD + rows) if up else slice(PAD, PAD + count)


def halo_rows(rows, count, up):
    return slice(PAD + rows, PAD + rows + count) if up else slice(PAD - count, PAD)


def doubled(values):
    return jnp.concatenate([values, values], axis=0)


def share_sent(step):
    return jnp.where(lax.axis_index("pitch") % (2 << step) == 1 << step, 0, 1)


def rebuild_shares(store_ref, times_ref, active_ref, share_ref, send_ref):
    harm_count = (store_ref.shape[1] - 1) // 2
    signals = store_ref.shape[2]
    active = doubled(active_ref[...])
    for which in range(2):
        angle = doubled(times_ref[which]).astype(F32) * period
        angle = angle - phase_lag if which == 0 else angle + phase_lag
        cos_1, sin_1 = jnp.cos(angle), jnp.sin(angle)
        cos_k, sin_k = cos_1, sin_1
        totals = [store_ref[which, 0, v] for v in range(signals)]
        for k in range(1, harm_count + 1):
            used = active >= k
            a, b = jnp.where(used, cos_k, 0.0), jnp.where(used, sin_k, 0.0)
            for v in range(signals):
                totals[v] = totals[v] + (
                    store_ref[which, k, v] * a + store_ref[which, harm_count + k, v] * b
                )
            cos_k, sin_k = cos_k * cos_1 - sin_k * sin_1, sin_k * cos_1 + cos_k * sin_1
        for v in range(signals):
            share_ref[which, v] = totals[v]
    send_ref[0] = share_ref[share_sent(0)]


def join_shares(step, share_ref, *refs):
    got_refs, out_ref = refs[:-1], refs[-1]
    out_ref[0] = share_ref[share_sent(step)]
    at = 1
    for got_ref in got_refs:
        out_ref[at : at + got_ref.shape[0]] = got_ref[...]
        at += got_ref.shape[0]


def join_ghosts(cells, rows, slabs, state_ref, source_ref, share_ref, *refs):
    got_refs, (ghost_ref, corner_ref) = refs[:-2], refs[-2:]
    refs = (state_ref, source_ref)
    part = rows // slabs
    pitch_at = lax.axis_index("pitch")
    blk_even = is_even("blk")
    corners, _ = corner_layout(state_ref.shape[0])

    for end in range(2):

        @pl.when(pitch_at == end * (slabs - 1))
        def _():
            pieces = [share_ref[end]]
            for got_ref in got_refs:
                pieces += [got_ref[i] for i in range(got_ref.shape[0])]
            for distance, piece in enumerate(pieces):
                at = part * (distance if end == 0 else slabs - 1 - distance)
                for layer in range(2):
                    ghost_ref[:, layer, at : at + part] = piece[:, layer * part : (layer + 1) * part]

            def write(up):
                for v, which, depth, count, place in corners:
                    if which == 0 and depth <= 2:
                        at = slice(rows - count, rows) if up else slice(0, count)
                        layer = depth - 1 if end else 2 - depth
                        corner_ref[place : place + count] = ghost_ref[v, layer, at]

            pl.when(blk_even)(lambda: write(False))
            pl.when(jnp.logical_not(blk_even))(lambda: write(True))

    @pl.when((pitch_at > 0) & (pitch_at < slabs - 1))
    def _():
        bottom = is_even("pitch")

        def write(up):
            for v, which, depth, count, place in corners:
                width = (HF, HP)[which]
                plane = jnp.where(bottom, width + depth - 1, width + cells - depth)
                corner_ref[place : place + count] = refs[which][v, plane, edge_rows(rows, count, up)]

        pl.when(blk_even)(lambda: write(False))
        pl.when(jnp.logical_not(blk_even))(lambda: write(True))


def prepare_close(store_ref, times_ref, active_ref, table_ref, base_ref, gain_ref):
    harm_count = (store_ref.shape[1] - 1) // 2
    signals = store_ref.shape[2]
    active = doubled(active_ref[...])
    gain = jnp.full(active.shape, relax_rate, F32)
    for k in range(1, harm_count + 1):
        gain = gain + jnp.where(active >= k, 2.0 * relax_rate * math.cos(k * phase_lag), 0.0)
    gain_ref[...] = gain
    keep = 1.0 - relax_rate
    for which in range(2):
        angle = doubled(times_ref[which]).astype(F32) * period + period
        cos_1, sin_1 = jnp.cos(angle), jnp.sin(angle)
        cos_k, sin_k = cos_1, sin_1
        totals = [store_ref[which, 0, v] for v in range(signals)]
        turn = -phase_lag if which == 0 else phase_lag
        for k in range(1, harm_count + 1):
            table_ref[which, k - 1] = (2.0 * relax_rate) * cos_k
            table_ref[which, harm_count + k - 1] = (2.0 * relax_rate) * sin_k
            used = active >= k
            c, s = math.cos(k * turn), math.sin(k * turn)
            a = jnp.where(used, cos_k * c - sin_k * s, 0.0)
            b = jnp.where(used, sin_k * c + cos_k * s, 0.0)
            for v in range(signals):
                totals[v] = totals[v] + (
                    store_ref[which, k, v] * a + store_ref[which, harm_count + k, v] * b
                )
            cos_k, sin_k = cos_k * cos_1 - sin_k * sin_1, sin_k * cos_1 + cos_k * sin_1
        for v in range(signals):
            base_ref[which, v] = keep * totals[v]


def edge_layout(variables, cells, reach):
    parts, place = [], 0
    for v in range(variables):
        for which, width in ((0, HF), (1, HP)):
            out = min(reach, width - 1)
            for plane in range(-out, cells + out):
                count = width - max(0, -plane, plane - cells + 1)
                parts.append((v, which, plane + width, count, place))
                place += count
    return parts, -(-place // 8) * 8


def corner_layout(variables):
    parts, place = [], 0
    for v in range(variables):
        for which, width in ((0, HF), (1, HP)):
            for depth in range(1, width):
                parts.append((v, which, depth, width - depth, place))
                place += width - depth
    return parts, -(-place // 8) * 8


def place_halos(cells, rows, slabs, *refs):
    first_ref, second_ref, edge_ref, corner_1, corner_2, ghost_ref = refs[2:8]
    state_ref, source_ref, out_ref = refs[-3:]
    refs = (state_ref, source_ref)
    pitch_at = lax.axis_index("pitch")
    even = is_even("pitch")
    blk_even = is_even("blk")
    variables = state_ref.shape[0]
    own_rows = slice(PAD, PAD + rows)
    for halo_ref, upper in ((first_ref, even), (second_ref, jnp.logical_not(even))):
        at = jnp.where(upper, HF + cells, 0)
        state_ref[:, pl.ds(at, HF), own_rows] = halo_ref[:, :HF]
        at = jnp.where(upper, HP + cells, 0)
        source_ref[:, pl.ds(at, HP), own_rows] = halo_ref[:, HF:]

    @pl.when(pitch_at == 0)
    def _():
        state_ref[:, HF - 2 : HF, own_rows] = ghost_ref[...]

    @pl.when(pitch_at == slabs - 1)
    def _():
        state_ref[:, HF + cells : HF + cells + 2, own_rows] = ghost_ref[...]

    edges, _ = edge_layout(variables, cells, 0)
    corners, _ = corner_layout(variables)
    parts, _ = edge_layout(variables, cells, HF)

    def move(up):
        for v, which, plane, count, place in parts:
            out_ref[place : place + count] = refs[which][v, plane, edge_rows(rows, count, not up)]
        for v, which, plane, count, place in edges:
            refs[which][v, plane, halo_rows(rows, count, up)] = edge_ref[place : place + count]
        for corner_ref, upper in ((corner_1, even), (corner_2, jnp.logical_not(even))):
            for v, which, depth, count, place in corners:
                width = (HF, HP)[which]
                plane = jnp.where(upper, width + cells + depth - 1, width - depth)
                refs[which][v, plane, halo_rows(rows, count, up)] = corner_ref[place : place + count]

    pl.when(blk_even)(lambda: move(False))
    pl.when(jnp.logical_not(blk_even))(lambda: move(True))


class Block:
    def __init__(self, cells, rows, slabs, blocks, state_ref, source_ref, flux_refs):
        self.cells, self.rows, self.slabs, self.blocks = cells, rows, slabs, blocks
        self.state_ref, self.source_ref, self.flux_refs = state_ref, source_ref, flux_refs
        self.variables, _, _, self.lanes = state_ref.shape
        self.pitch_at = lax.axis_index("pitch")
        self.blk_at = lax.axis_index("blk")

    def clamp_ends(self, ref):
        rows = self.rows
        shape = (self.variables, ref.shape[1], 2, self.lanes)

        @pl.when(self.blk_at == 0)
        def _():
            ref[:, :, PAD - 2 : PAD] = jnp.broadcast_to(ref[:, :, PAD : PAD + 1], shape)

        @pl.when(self.blk_at == self.blocks - 1)
        def _():
            ref[:, :, PAD + rows : PAD + rows + 2] = jnp.broadcast_to(
                ref[:, :, PAD + rows - 1 : PAD + rows], shape
            )

    def keep_ghosts(self, ref, width):
        for end, at in ((0, 0), (self.slabs - 1, 2 + self.cells)):

            @pl.when(self.pitch_at == end)
            def _():
                ref[:, width - 2 + at : width + at] = self.state_ref[:, HF - 2 + at : HF + at]

    def shift_down(self, values, lane):
        return jnp.where(lane == self.lanes - 1, values, pltpu.roll(values, self.lanes - 1, 1))

    def shift_up(self, values, lane):
        return jnp.where(lane == 0, values, pltpu.roll(values, 1, 1))

    def advance(self, step, from_ref, to_ref, lo, hi):
        width = HF - 2 * step
        out_width = width - 2
        last = step == len(section_coefs) - 1
        scale = section_coefs[step] * pseudo_step
        count = -(-(self.rows + 2 * out_width) // 8) * 8
        row_at = PAD - out_width
        variables, lanes = self.variables, self.lanes
        pitch_ref, axial_ref, radial_ref = self.flux_refs

        def fluxes(plane):
            u = [from_ref[v, plane + width] for v in range(variables)]
            inverse = 1.0 / u[0]
            speed = [u[d] * inverse for d in (1, 2, 3)]
            pressure = gamma_less * (
                u[4] - 0.5 * (u[1] * speed[0] + u[2] * speed[1] + u[3] * speed[2])
            )
            half = (0.5 * scale) * pressure
            total = u[4] + pressure
            for d, flux_ref in enumerate((pitch_ref, axial_ref, radial_ref)):
                w = (0.5 * scale) * speed[d]
                for v in (1, 2, 3):
                    flux = u[v] * w
                    flux_ref[v - 1, plane + HP + 1] = flux + half if v == d + 1 else flux
                flux_ref[3, plane + HP + 1] = total * w

        def update(plane):
            lane = lax.broadcasted_iota(jnp.int32, (count, lanes), 1)
            for v in range(variables):

                def state(ahead, over):
                    return from_ref[v, plane + width + ahead, row_at + over : row_at + over + count]

                def change_of(ref, d, ahead, over):
                    def flux(sign):
                        at = row_at + sign * over
                        at = slice(at, at + count)
                        if v == 0:
                            return from_ref[d, plane + width + sign * ahead, at]
                        return ref[v - 1, plane + HP + 1 + sign * ahead, at]

                    return flux(1) - flux(-1)

                here = state(0, 0)
                change = change_of(pitch_ref, 1, 1, 0) + change_of(axial_ref, 2, 0, 1)
                along = from_ref[3, plane + width, row_at : row_at + count] if v == 0 else (
                    radial_ref[v - 1, plane + HP + 1, row_at : row_at + count]
                )
                if v == 0:
                    change = (0.5 * scale) * change
                    along = (0.5 * scale) * along
                near = (state(1, 0) + state(-1, 0)) + (state(0, 1) + state(0, -1))
                far = (state(2, 0) + state(-2, 0)) + (state(0, 2) + state(0, -2))
                scaled = (scale * diss_coeff) * here
                near_here = 4.0 * scaled
                ahead = self.shift_down(near_here + along - self.shift_down(scaled, lane), lane)
                behind = self.shift_up(near_here - along - self.shift_up(scaled, lane), lane)
                change = change + (ahead + behind) + (scale * diss_coeff) * (4.0 * near - far)
                change = change + (scale * (1.5 / physical_step - 18.0 * diss_coeff)) * here
                source = self.source_ref[v, plane + HP, row_at : row_at + count]
                flow = self.state_ref[v, plane + HF, row_at : row_at + count]
                to_at = row_at - PAD if last else row_at
                to_ref[v, plane + out_width, to_at : to_at + count] = (flow + scale * source) - change

        def pairs(body, start, stop):
            def both(index, carry):
                plane = start + 2 * index
                body(plane)
                body(plane + 1)
                return carry

            lax.fori_loop(0, (stop - start) // 2, both, 0)

        pairs(fluxes, lo - 1, hi + 1)
        pairs(update, lo, hi)
        if not last:
            self.clamp_ends(to_ref)


def start_sections(cells, rows, slabs, blocks, *refs):
    got_ref = refs[2]
    state_ref, source_ref, mid_1, mid_2, new_ref, own_ref = refs[3:9]
    send_refs, flux_refs = refs[9 : 8 + slabs], refs[8 + slabs :]
    block = Block(cells, rows, slabs, blocks, state_ref, source_ref, flux_refs)
    variables = state_ref.shape[0]
    parts, _ = edge_layout(variables, cells, HF)
    into = (state_ref, source_ref)

    def unpack(up):
        for v, which, plane, count, place in parts:
            into[which][v, plane, halo_rows(rows, count, up)] = got_ref[place : place + count]

    pl.when(is_even("blk"))(lambda: unpack(True))
    pl.when(jnp.logical_not(is_even("blk")))(lambda: unpack(False))
    block.clamp_ends(state_ref)
    block.keep_ghosts(mid_1, HF - 2)
    block.keep_ghosts(mid_2, HF - 4)
    part = rows // slabs
    high = block.pitch_at == slabs - 1

    @pl.when((block.pitch_at == 0) | high)
    def _():
        for step, (from_ref, to_ref) in enumerate(
            ((state_ref, mid_1), (mid_1, mid_2), (mid_2, new_ref))
        ):
            planes = HF - 2 * step
            lo = jnp.where(high, cells - planes, 0)
            block.advance(step, from_ref, to_ref, lo, lo + planes)

    for end, plane in ((0, 0), (slabs - 1, cells - 2)):

        @pl.when(block.pitch_at == end)
        def _():
            for j, out_ref in enumerate((own_ref,) + tuple(send_refs)):
                at = (end ^ j) * part
                for layer in range(2):
                    out_ref[:, layer * part : (layer + 1) * part] = new_ref[
                        :, plane + layer, at : at + part
                    ]


def finish_sections(cells, rows, slabs, blocks, *refs):
    state_ref, source_ref = refs[:2]
    mid_1, mid_2, new_ref = refs[5:8]
    block = Block(cells, rows, slabs, blocks, state_ref, source_ref, refs[8:])
    low, high = block.pitch_at == 0, block.pitch_at == slabs - 1
    for step, (from_ref, to_ref) in enumerate(
        ((state_ref, mid_1), (mid_1, mid_2), (mid_2, new_ref))
    ):
        done = HF - 2 * step
        out_width = done - 2
        lo = jnp.where(low, done, -out_width)
        hi = jnp.where(high, cells - done, cells + out_width)
        block.advance(step, from_ref, to_ref, lo, hi)


def close(chunks, *refs):
    new_ref, store_ref, table_ref, base_ref, gain_ref, own_ref = refs[:6]
    got_refs = refs[6:-5]
    state_hbm, out_ref, ghost_ref, fresh_ref, sems = refs[-5:]
    slabs = len(got_refs) + 1
    at = lax.axis_index("pitch")
    copies = []

    def send(from_ref, to_ref):
        copy = pltpu.make_async_copy(from_ref, to_ref, sems.at[len(copies)])
        copy.start()
        copies.append(copy)

    send(new_ref, state_hbm)
    top, bottom = own_ref[...], own_ref[...]
    for j in range(1, slabs):
        got = got_refs[j - 1][...]
        top = jnp.where(at == slabs - 1 - j, got, top)
        bottom = jnp.where(at == j, got, bottom)
    keep = 1.0 - relax_rate
    signals = store_ref.shape[2]
    for which, sample in enumerate((top, bottom)):
        for lo, hi in zip(chunks[:-1], chunks[1:]):
            for k in range(lo, hi):
                weight = relax_rate if k == 0 else table_ref[which, k - 1]
                for v in range(signals):
                    fresh_ref[which, k, v] = keep * store_ref[which, k, v] + weight * sample[v]
            window = pl.ds(lo, hi - lo)
            send(fresh_ref.at[which, window], out_ref.at[which, window])
        ghost_ref[which] = base_ref[which] + sample * gain_ref[...][None]
    for copy in copies:
        copy.wait()


def swap_pairs(count, start):
    pairs = [(i, i + 1) for i in range(start, count - 1, 2)]
    return pairs + [(b, a) for a, b in pairs]


def flip_pairs(count, bits):
    return [(i, i ^ bits) for i in range(count)]


def diagonal_pairs(slabs, blocks, start):
    along = dict((i, i) for i in range(slabs))
    along.update(swap_pairs(slabs, start))
    return [
        (b * slabs + p, other * slabs + along[p])
        for b, other in swap_pairs(blocks, 1)
        for p in range(slabs)
    ]


def shards(flow_state, prior_state, fourier_store, sample_times, harmonics):
    slabs = lax.axis_size("pitch")
    blocks = lax.axis_size("blk")
    variables, cells, rows, lanes = flow_state.shape
    orders, signals, part = fourier_store.shape[1:4]
    store = fourier_store.reshape(2, orders, variables, 2 * part, lanes)
    halo = (variables, HF + HP, rows, lanes)
    face = (variables, 2 * part, lanes)
    long_rows = rows + 2 * PAD
    state_shape = (variables, cells + 2 * HF, long_rows, lanes)
    source_shape = (variables, cells + 2 * HP, long_rows, lanes)
    corner = (corner_layout(variables)[1], lanes)

    state, source, first, second = call(
        start_block,
        [state_shape, source_shape, halo, halo],
        pltpu.with_memory_space_constraint(flow_state, pltpu.MemorySpace.HBM),
        pltpu.with_memory_space_constraint(prior_state, pltpu.MemorySpace.HBM),
        scratch=[pltpu.VMEM(flow_state.shape, F32), pltpu.SemaphoreType.DMA((2,))],
        in_specs=[HBM, HBM],
        cost=1,
    )
    first = lax.ppermute(first, "pitch", swap_pairs(slabs, 0))
    second = lax.ppermute(second, "pitch", swap_pairs(slabs, 1))

    share, send = call(
        rebuild_shares, [(2,) + face, (1,) + face], store, sample_times, harmonics
    )
    gathered, step = [lax.ppermute(send, "pitch", flip_pairs(slabs, 1))], 1
    edge, corner_1 = call(
        functools.partial(pack_axial, cells, rows),
        [(edge_layout(variables, cells, 0)[1], lanes), corner],
        state,
        source,
    )
    edge = lax.ppermute(edge, "blk", swap_pairs(blocks, 1))
    corner_1 = lax.ppermute(corner_1, ("blk", "pitch"), diagonal_pairs(slabs, blocks, 0))
    while 1 << step < slabs:
        [send] = call(
            functools.partial(join_shares, step), [(1 << step,) + face], share, *gathered
        )
        gathered.append(lax.ppermute(send, "pitch", flip_pairs(slabs, 1 << step)))
        step += 1
    ghost, corner_2 = call(
        functools.partial(join_ghosts, cells, rows, slabs),
        [(variables, 2, rows, lanes), corner],
        state,
        source,
        share,
        *gathered,
    )
    corner_2 = lax.ppermute(corner_2, ("blk", "pitch"), diagonal_pairs(slabs, blocks, 1))
    table, base, gain = call(
        prepare_close,
        [(2, orders - 1, 2 * part, lanes), (2,) + face, (2 * part, lanes)],
        store,
        sample_times,
        harmonics,
    )

    state, source, out = call(
        functools.partial(place_halos, cells, rows, slabs),
        [state_shape, source_shape, (edge_layout(variables, cells, HF)[1], lanes)],
        state,
        source,
        first,
        second,
        edge,
        corner_1,
        corner_2,
        ghost,
        gain,
        aliases={0: 0, 1: 1},
    )
    got = lax.ppermute(out, "blk", swap_pairs(blocks, 0))
    mid_shapes = [
        (variables, cells + 2 * HP, long_rows, lanes),
        (variables, cells + 2 * HP - 4, long_rows, lanes),
    ]
    flux_shape = (variables - 1, cells + 2 * HP + 2, long_rows, lanes)
    flux_scratch = [pltpu.VMEM(flux_shape, F32)] * 3
    sizes = (cells, rows, slabs, blocks)
    state, source, mid_1, mid_2, new, own, *sends = call(
        functools.partial(start_sections, *sizes),
        [state_shape, source_shape] + mid_shapes + [flow_state.shape] + [face] * slabs,
        state,
        source,
        got,
        scratch=flux_scratch,
        aliases={0: 0, 1: 1},
        limit=12,
    )
    samples = [None] * (slabs - 1)
    for j in range(slabs - 1, 0, -1):
        samples[j - 1] = lax.ppermute(
            sends[j - 1], "pitch", [(0, j), (slabs - 1, slabs - 1 - j)]
        )
    _, _, new = call(
        functools.partial(finish_sections, *sizes),
        mid_shapes + [flow_state.shape],
        state,
        source,
        mid_1,
        mid_2,
        new,
        scratch=flux_scratch,
        aliases={2: 0, 3: 1, 4: 2},
        limit=12,
    )
    pieces = 7
    chunks = [orders * i // pieces for i in range(pieces + 1)]
    new_state, new_store, new_ghosts = call(
        functools.partial(close, chunks),
        [flow_state.shape, store.shape, (2,) + face],
        new,
        store,
        table,
        base,
        gain,
        own,
        *samples,
        scratch=[pltpu.VMEM(store.shape, F32), pltpu.SemaphoreType.DMA((2 * pieces + 1,))],
        out_specs=[HBM, HBM, VMEM],
    )
    return (
        new_state,
        new_store.reshape(fourier_store.shape),
        new_ghosts.reshape(2, signals, part, lanes),
    )


def solution(mesh):
    placed = (
        P(None, "pitch", "blk", None),
        P(None, "pitch", "blk", None),
        P(None, None, None, ("blk", "pitch"), None),
        P(None, ("blk", "pitch"), None),
        P(("blk", "pitch"), None),
    )
    return jax.shard_map(
        shards,
        mesh=mesh,
        in_specs=placed,
        out_specs=(
            P(None, "pitch", "blk", None),
            P(None, None, None, ("blk", "pitch"), None),
            P(None, None, ("blk", "pitch"), None),
        ),
        check_vma=False,
    )
```

```python
import functools
import math

import jax
import jax.numpy as jnp
from jax import lax
from jax.experimental import pallas as pl
from jax.experimental.pallas import tpu as pltpu
from jax.sharding import PartitionSpec as P


NT = 96

gamma_less = 0.4
diss_coeff = 0.03125
section_coefs = (1.0 / 3.0, 0.5, 1.0)
pseudo_step = 0.1
physical_step = 0.25
relax_rate = 0.125
lag_turns = 0.3
period = 2.0 * math.pi / NT
phase_lag = 2.0 * math.pi * lag_turns

HF = 2 * len(section_coefs)
HP = HF - 2
PAD = 8

F32 = jnp.float32
VMEM = pl.BlockSpec(memory_space=pltpu.VMEM)


HBM = pl.BlockSpec(memory_space=pltpu.MemorySpace.HBM)


def call(body, outs, *args, scratch=(), aliases=None, in_specs=None, out_specs=None, types=None, cost=0, limit=8):
    outs = [jax.ShapeDtypeStruct(shape, kind) for shape, kind in zip(outs, types or [F32] * len(outs))]
    moved = 4 * sum(math.prod(a.shape) for a in list(args) + outs)
    return pl.pallas_call(
        body,
        out_shape=outs,
        in_specs=in_specs or [VMEM] * len(args),
        out_specs=out_specs or [VMEM] * len(outs),
        scratch_shapes=list(scratch),
        input_output_aliases=aliases or {},
        compiler_params=pltpu.CompilerParams(vmem_limit_bytes=limit << 20),
        cost_estimate=pl.CostEstimate(flops=cost, bytes_accessed=moved, transcendentals=0),
    )(*args)


def is_even(axis):
    return lax.axis_index(axis) % 2 == 0


def source_of(flow, prior):
    return (2.0 / physical_step) * flow - (0.5 / physical_step) * prior


def pack_pitch(cells, rows, state_ref, prior_ref, source_ref, first_ref, second_ref):
    own_rows = slice(PAD, PAD + rows)
    even = is_even("pitch")
    source_ref[:, HP : HP + cells, own_rows] = source_of(
        state_ref[:, HF : HF + cells, own_rows], prior_ref[...]
    )
    for out_ref, top in ((first_ref, even), (second_ref, jnp.logical_not(even))):
        at = jnp.where(top, cells, HF)
        out_ref[:, :HF] = state_ref[:, pl.ds(at, HF), own_rows]
        at = jnp.where(top, cells, HP)
        out_ref[:, HF:] = source_ref[:, pl.ds(at, HP), own_rows]


def pack_axial(cells, rows, state_ref, source_ref, edge_ref, corner_ref):
    refs = (state_ref, source_ref)
    edges, _ = edge_layout(state_ref.shape[0], cells, 0)
    corners, _ = corner_layout(state_ref.shape[0])
    top = is_even("pitch")

    def write(up):
        for v, which, plane, count, place in edges:
            edge_ref[place : place + count] = refs[which][v, plane, edge_rows(rows, count, up)]
        for v, which, depth, count, place in corners:
            width = (HF, HP)[which]
            plane = jnp.where(top, width + cells - depth, width + depth - 1)
            corner_ref[place : place + count] = refs[which][v, plane, edge_rows(rows, count, up)]

    @pl.when(is_even("blk"))
    def _():
        write(False)

    @pl.when(jnp.logical_not(is_even("blk")))
    def _():
        write(True)


def edge_rows(rows, count, up):
    return slice(PAD + rows - count, PAD + rows) if up else slice(PAD, PAD + count)


def halo_rows(rows, count, up):
    return slice(PAD + rows, PAD + rows + count) if up else slice(PAD - count, PAD)


def doubled(values):
    return jnp.concatenate([values, values], axis=0)


def share_sent(step):
    return jnp.where(lax.axis_index("pitch") % (2 << step) == 1 << step, 0, 1)


def rebuild_shares(*refs):
    store_hbm, times_hbm, active_hbm, flow_hbm, prior_hbm = refs[:5]
    store_ref, times_ref, active_ref, state_ref, prior_ref, share_ref, send_ref, sems = refs[5:]
    cells, rows = flow_hbm.shape[1:3]
    copies = [
        pltpu.make_async_copy(from_ref, to_ref, sems.at[i])
        for i, (from_ref, to_ref) in enumerate(
            (
                (times_hbm, times_ref),
                (active_hbm, active_ref),
                (store_hbm.at[0], store_ref.at[0]),
                (store_hbm.at[1], store_ref.at[1]),
                (flow_hbm, state_ref.at[:, pl.ds(HF, cells), pl.ds(PAD, rows)]),
                (prior_hbm, prior_ref),
            )
        )
    ]
    for copy in copies:
        copy.start()
    copies[0].wait()
    copies[1].wait()
    harm_count = (store_ref.shape[1] - 1) // 2
    signals = store_ref.shape[2]
    active = doubled(active_ref[...])
    for which in range(2):
        angle = doubled(times_ref[which]).astype(F32) * period
        angle = angle - phase_lag if which == 0 else angle + phase_lag
        cos_1, sin_1 = jnp.cos(angle), jnp.sin(angle)
        copies[2 + which].wait()
        cos_k, sin_k = cos_1, sin_1
        totals = [store_ref[which, 0, v] for v in range(signals)]
        for k in range(1, harm_count + 1):
            used = active >= k
            a, b = jnp.where(used, cos_k, 0.0), jnp.where(used, sin_k, 0.0)
            for v in range(signals):
                totals[v] = totals[v] + (
                    store_ref[which, k, v] * a + store_ref[which, harm_count + k, v] * b
                )
            cos_k, sin_k = cos_k * cos_1 - sin_k * sin_1, sin_k * cos_1 + cos_k * sin_1
        for v in range(signals):
            share_ref[which, v] = totals[v]
    send_ref[0] = share_ref[share_sent(0)]
    copies[4].wait()
    copies[5].wait()


def join_shares(step, share_ref, *refs):
    got_refs, out_ref = refs[:-1], refs[-1]
    out_ref[0] = share_ref[share_sent(step)]
    at = 1
    for got_ref in got_refs:
        out_ref[at : at + got_ref.shape[0]] = got_ref[...]
        at += got_ref.shape[0]


def join_ghosts(cells, rows, slabs, state_ref, source_ref, share_ref, *refs):
    got_refs, (ghost_ref, corner_ref) = refs[:-2], refs[-2:]
    refs = (state_ref, source_ref)
    part = rows // slabs
    pitch_at = lax.axis_index("pitch")
    blk_even = is_even("blk")
    corners, _ = corner_layout(state_ref.shape[0])

    for end in range(2):

        @pl.when(pitch_at == end * (slabs - 1))
        def _():
            pieces = [share_ref[end]]
            for got_ref in got_refs:
                pieces += [got_ref[i] for i in range(got_ref.shape[0])]
            for distance, piece in enumerate(pieces):
                at = part * (distance if end == 0 else slabs - 1 - distance)
                for layer in range(2):
                    ghost_ref[:, layer, at : at + part] = piece[:, layer * part : (layer + 1) * part]

            def write(up):
                for v, which, depth, count, place in corners:
                    if which == 0 and depth <= 2:
                        at = slice(rows - count, rows) if up else slice(0, count)
                        layer = depth - 1 if end else 2 - depth
                        corner_ref[place : place + count] = ghost_ref[v, layer, at]

            pl.when(blk_even)(lambda: write(False))
            pl.when(jnp.logical_not(blk_even))(lambda: write(True))

    @pl.when((pitch_at > 0) & (pitch_at < slabs - 1))
    def _():
        bottom = is_even("pitch")

        def write(up):
            for v, which, depth, count, place in corners:
                width = (HF, HP)[which]
                plane = jnp.where(bottom, width + depth - 1, width + cells - depth)
                corner_ref[place : place + count] = refs[which][v, plane, edge_rows(rows, count, up)]

        pl.when(blk_even)(lambda: write(False))
        pl.when(jnp.logical_not(blk_even))(lambda: write(True))


def prepare_close(store_ref, times_ref, active_ref, table_ref, base_ref, gain_ref):
    harm_count = (store_ref.shape[1] - 1) // 2
    signals = store_ref.shape[2]
    active = doubled(active_ref[...])
    gain = jnp.full(active.shape, relax_rate, F32)
    for k in range(1, harm_count + 1):
        gain = gain + jnp.where(active >= k, 2.0 * relax_rate * math.cos(k * phase_lag), 0.0)
    gain_ref[...] = gain
    keep = 1.0 - relax_rate
    for which in range(2):
        angle = doubled(times_ref[which]).astype(F32) * period + period
        cos_1, sin_1 = jnp.cos(angle), jnp.sin(angle)
        cos_k, sin_k = cos_1, sin_1
        totals = [store_ref[which, 0, v] for v in range(signals)]
        turn = -phase_lag if which == 0 else phase_lag
        for k in range(1, harm_count + 1):
            table_ref[which, k - 1] = (2.0 * relax_rate) * cos_k
            table_ref[which, harm_count + k - 1] = (2.0 * relax_rate) * sin_k
            used = active >= k
            c, s = math.cos(k * turn), math.sin(k * turn)
            a = jnp.where(used, cos_k * c - sin_k * s, 0.0)
            b = jnp.where(used, sin_k * c + cos_k * s, 0.0)
            for v in range(signals):
                totals[v] = totals[v] + (
                    store_ref[which, k, v] * a + store_ref[which, harm_count + k, v] * b
                )
            cos_k, sin_k = cos_k * cos_1 - sin_k * sin_1, sin_k * cos_1 + cos_k * sin_1
        for v in range(signals):
            base_ref[which, v] = keep * totals[v]


def edge_layout(variables, cells, reach):
    parts, place = [], 0
    for v in range(variables):
        for which, width in ((0, HF), (1, HP)):
            out = min(reach, width - 1)
            for plane in range(-out, cells + out):
                count = width - max(0, -plane, plane - cells + 1)
                parts.append((v, which, plane + width, count, place))
                place += count
    return parts, -(-place // 8) * 8


def corner_layout(variables):
    parts, place = [], 0
    for v in range(variables):
        for which, width in ((0, HF), (1, HP)):
            for depth in range(1, width):
                parts.append((v, which, depth, width - depth, place))
                place += width - depth
    return parts, -(-place // 8) * 8


def place_halos(cells, rows, slabs, *refs):
    first_ref, second_ref, edge_ref, corner_1, corner_2, ghost_ref = refs[2:8]
    state_ref, source_ref, out_ref = refs[-3:]
    refs = (state_ref, source_ref)
    pitch_at = lax.axis_index("pitch")
    even = is_even("pitch")
    blk_even = is_even("blk")
    variables = state_ref.shape[0]
    own_rows = slice(PAD, PAD + rows)
    for halo_ref, upper in ((first_ref, even), (second_ref, jnp.logical_not(even))):
        at = jnp.where(upper, HF + cells, 0)
        state_ref[:, pl.ds(at, HF), own_rows] = halo_ref[:, :HF]
        at = jnp.where(upper, HP + cells, 0)
        source_ref[:, pl.ds(at, HP), own_rows] = halo_ref[:, HF:]

    @pl.when(pitch_at == 0)
    def _():
        state_ref[:, HF - 2 : HF, own_rows] = ghost_ref[...]

    @pl.when(pitch_at == slabs - 1)
    def _():
        state_ref[:, HF + cells : HF + cells + 2, own_rows] = ghost_ref[...]

    edges, _ = edge_layout(variables, cells, 0)
    corners, _ = corner_layout(variables)
    parts, _ = edge_layout(variables, cells, HF)

    def move(up):
        for v, which, plane, count, place in parts:
            out_ref[place : place + count] = refs[which][v, plane, edge_rows(rows, count, not up)]
        for v, which, plane, count, place in edges:
            refs[which][v, plane, halo_rows(rows, count, up)] = edge_ref[place : place + count]
        for corner_ref, upper in ((corner_1, even), (corner_2, jnp.logical_not(even))):
            for v, which, depth, count, place in corners:
                width = (HF, HP)[which]
                plane = jnp.where(upper, width + cells + depth - 1, width - depth)
                refs[which][v, plane, halo_rows(rows, count, up)] = corner_ref[place : place + count]

    pl.when(blk_even)(lambda: move(False))
    pl.when(jnp.logical_not(blk_even))(lambda: move(True))


class Block:
    def __init__(self, cells, rows, slabs, blocks, state_ref, source_ref, flux_refs):
        self.cells, self.rows, self.slabs, self.blocks = cells, rows, slabs, blocks
        self.state_ref, self.source_ref, self.flux_refs = state_ref, source_ref, flux_refs
        self.variables, _, _, self.lanes = state_ref.shape
        self.pitch_at = lax.axis_index("pitch")
        self.blk_at = lax.axis_index("blk")

    def clamp_ends(self, ref):
        rows = self.rows
        shape = (self.variables, ref.shape[1], 2, self.lanes)

        @pl.when(self.blk_at == 0)
        def _():
            ref[:, :, PAD - 2 : PAD] = jnp.broadcast_to(ref[:, :, PAD : PAD + 1], shape)

        @pl.when(self.blk_at == self.blocks - 1)
        def _():
            ref[:, :, PAD + rows : PAD + rows + 2] = jnp.broadcast_to(
                ref[:, :, PAD + rows - 1 : PAD + rows], shape
            )

    def keep_ghosts(self, ref, width):
        for end, at in ((0, 0), (self.slabs - 1, 2 + self.cells)):

            @pl.when(self.pitch_at == end)
            def _():
                ref[:, width - 2 + at : width + at] = self.state_ref[:, HF - 2 + at : HF + at]

    def shift_down(self, values, lane):
        return jnp.where(lane == self.lanes - 1, values, pltpu.roll(values, self.lanes - 1, 1))

    def shift_up(self, values, lane):
        return jnp.where(lane == 0, values, pltpu.roll(values, 1, 1))

    def advance(self, step, from_ref, to_ref, lo, hi):
        width = HF - 2 * step
        out_width = width - 2
        last = step == len(section_coefs) - 1
        scale = section_coefs[step] * pseudo_step
        count = -(-(self.rows + 2 * out_width) // 8) * 8
        row_at = PAD - out_width
        variables, lanes = self.variables, self.lanes
        pitch_ref, axial_ref, radial_ref = self.flux_refs

        def fluxes(plane):
            u = [from_ref[v, plane + width] for v in range(variables)]
            inverse = 1.0 / u[0]
            speed = [u[d] * inverse for d in (1, 2, 3)]
            pressure = gamma_less * (
                u[4] - 0.5 * (u[1] * speed[0] + u[2] * speed[1] + u[3] * speed[2])
            )
            half = (0.5 * scale) * pressure
            total = u[4] + pressure
            for d, flux_ref in enumerate((pitch_ref, axial_ref, radial_ref)):
                w = (0.5 * scale) * speed[d]
                for v in (1, 2, 3):
                    flux = u[v] * w
                    flux_ref[v - 1, plane + HP + 1] = flux + half if v == d + 1 else flux
                flux_ref[3, plane + HP + 1] = total * w

        def update(plane):
            lane = lax.broadcasted_iota(jnp.int32, (count, lanes), 1)
            for v in range(variables):

                def state(ahead, over):
                    return from_ref[v, plane + width + ahead, row_at + over : row_at + over + count]

                def change_of(ref, d, ahead, over):
                    def flux(sign):
                        at = row_at + sign * over
                        at = slice(at, at + count)
                        if v == 0:
                            return from_ref[d, plane + width + sign * ahead, at]
                        return ref[v - 1, plane + HP + 1 + sign * ahead, at]

                    return flux(1) - flux(-1)

                here = state(0, 0)
                change = change_of(pitch_ref, 1, 1, 0) + change_of(axial_ref, 2, 0, 1)
                along = from_ref[3, plane + width, row_at : row_at + count] if v == 0 else (
                    radial_ref[v - 1, plane + HP + 1, row_at : row_at + count]
                )
                if v == 0:
                    change = (0.5 * scale) * change
                    along = (0.5 * scale) * along
                near = (state(1, 0) + state(-1, 0)) + (state(0, 1) + state(0, -1))
                far = (state(2, 0) + state(-2, 0)) + (state(0, 2) + state(0, -2))
                scaled = (scale * diss_coeff) * here
                near_here = 4.0 * scaled
                ahead = self.shift_down(near_here + along - self.shift_down(scaled, lane), lane)
                behind = self.shift_up(near_here - along - self.shift_up(scaled, lane), lane)
                change = change + (ahead + behind) + (scale * diss_coeff) * (4.0 * near - far)
                change = change + (scale * (1.5 / physical_step - 18.0 * diss_coeff)) * here
                source = self.source_ref[v, plane + HP, row_at : row_at + count]
                flow = self.state_ref[v, plane + HF, row_at : row_at + count]
                to_at = row_at - PAD if last else row_at
                to_ref[v, plane + out_width, to_at : to_at + count] = (flow + scale * source) - change

        def pairs(body, start, stop):
            def both(index, carry):
                plane = start + 2 * index
                body(plane)
                body(plane + 1)
                return carry

            lax.fori_loop(0, (stop - start) // 2, both, 0)

        pairs(fluxes, lo - 1, hi + 1)
        pairs(update, lo, hi)
        if not last:
            self.clamp_ends(to_ref)


def start_sections(cells, rows, slabs, blocks, *refs):
    got_ref = refs[2]
    state_ref, source_ref, mid_1, mid_2, new_ref, kept_ref, sent_ref = refs[3:10]
    flux_refs = refs[10:]
    block = Block(cells, rows, slabs, blocks, state_ref, source_ref, flux_refs)
    variables = state_ref.shape[0]
    parts, _ = edge_layout(variables, cells, HF)
    into = (state_ref, source_ref)

    def unpack(up):
        for v, which, plane, count, place in parts:
            into[which][v, plane, halo_rows(rows, count, up)] = got_ref[place : place + count]

    pl.when(is_even("blk"))(lambda: unpack(True))
    pl.when(jnp.logical_not(is_even("blk")))(lambda: unpack(False))
    block.clamp_ends(state_ref)
    block.keep_ghosts(mid_1, HF - 2)
    block.keep_ghosts(mid_2, HF - 4)
    part = rows // slabs
    high = block.pitch_at == slabs - 1

    @pl.when((block.pitch_at == 0) | high)
    def _():
        for step, (from_ref, to_ref) in enumerate(
            ((state_ref, mid_1), (mid_1, mid_2), (mid_2, new_ref))
        ):
            planes = HF - 2 * step
            lo = jnp.where(high, cells - planes, 0)
            block.advance(step, from_ref, to_ref, lo, lo + planes)

    for end, plane in ((0, 0), (slabs - 1, cells - 2)):

        @pl.when(block.pitch_at == end)
        def _():
            for j in range(slabs):
                out_ref, i = (kept_ref, j) if 2 * j < slabs else (sent_ref, j - slabs // 2)
                at = (end ^ j) * part
                for layer in range(2):
                    out_ref[i, :, layer * part : (layer + 1) * part] = new_ref[
                        :, plane + layer, at : at + part
                    ]


def finish_sections(cells, rows, slabs, blocks, *refs):
    state_ref, source_ref = refs[:2]
    mid_1, mid_2, new_ref = refs[5:8]
    block = Block(cells, rows, slabs, blocks, state_ref, source_ref, refs[8:])
    low, high = block.pitch_at == 0, block.pitch_at == slabs - 1
    for step, (from_ref, to_ref) in enumerate(
        ((state_ref, mid_1), (mid_1, mid_2), (mid_2, new_ref))
    ):
        done = HF - 2 * step
        out_width = done - 2
        lo = jnp.where(low, done, -out_width)
        hi = jnp.where(high, cells - done, cells + out_width)
        block.advance(step, from_ref, to_ref, lo, hi)


def pass_on(step, held_ref, got_ref, after_ref, kept_ref, sent_ref):
    del after_ref
    at = lax.axis_index("pitch") % (2 << step)
    half = kept_ref.shape[0]
    got = (at == 1 << step) | (at == (1 << step) - 1)

    @pl.when(got)
    def _():
        kept_ref[...] = got_ref[:half]
        sent_ref[...] = got_ref[half:]

    @pl.when(jnp.logical_not(got))
    def _():
        kept_ref[...] = held_ref[:half]
        sent_ref[...] = held_ref[half:]


def refresh_half(pieces, which, sample_ref, store_ref, table_ref, fresh_ref, out_ref, send):
    keep = 1.0 - relax_rate
    sample = [sample_ref[0, v] for v in range(store_ref.shape[2])]
    for lo, hi in zip(pieces[:-1], pieces[1:]):
        for k in range(lo, hi):
            weight = relax_rate if k == 0 else table_ref[which, k - 1]
            for v, value in enumerate(sample):
                fresh_ref[k, v] = keep * store_ref[which, k, v] + weight * value
        window = pl.ds(lo, hi - lo)
        send(fresh_ref.at[window], out_ref.at[which, window])


def sender(sems):
    copies = []

    def send(from_ref, to_ref):
        copy = pltpu.make_async_copy(from_ref, to_ref, sems.at[len(copies)])
        copy.start()
        copies.append(copy)

    return copies, send


def close_first(pieces, new_ref, store_ref, table_ref, sample_ref, state_hbm, out_ref, fresh_ref, sems):
    copies, send = sender(sems)
    send(new_ref, state_hbm)
    which = 1 - lax.axis_index("pitch") % 2
    refresh_half(pieces, which, sample_ref, store_ref, table_ref, fresh_ref, out_ref, send)
    for copy in copies:
        copy.wait()


def close_second(pieces, *refs):
    store_ref, table_ref, base_ref, gain_ref, first_ref, second_ref = refs[1:7]
    out_ref, ghost_hbm, fresh_ref, ghost_ref, sems = refs[7:]
    copies, send = sender(sems)
    which = lax.axis_index("pitch") % 2
    gain = gain_ref[...]
    for at, sample_ref in ((1 - which, first_ref), (which, second_ref)):
        ghost_ref[at] = base_ref[at] + sample_ref[0] * gain[None]
    send(ghost_ref, ghost_hbm)
    refresh_half(pieces, which, second_ref, store_ref, table_ref, fresh_ref, out_ref, send)
    for copy in copies:
        copy.wait()


def swap_pairs(count, start):
    pairs = [(i, i + 1) for i in range(start, count - 1, 2)]
    return pairs + [(b, a) for a, b in pairs]


def flip_pairs(count, bits):
    return [(i, i ^ bits) for i in range(count)]


def diagonal_pairs(slabs, blocks, start):
    along = dict((i, i) for i in range(slabs))
    along.update(swap_pairs(slabs, start))
    return [
        (b * slabs + p, other * slabs + along[p])
        for b, other in swap_pairs(blocks, 1)
        for p in range(slabs)
    ]


def shards(flow_state, prior_state, fourier_store, sample_times, harmonics):
    slabs = lax.axis_size("pitch")
    blocks = lax.axis_size("blk")
    variables, cells, rows, lanes = flow_state.shape
    orders, signals, part = fourier_store.shape[1:4]
    store = fourier_store.reshape(2, orders, variables, 2 * part, lanes)
    halo = (variables, HF + HP, rows, lanes)
    face = (variables, 2 * part, lanes)
    long_rows = rows + 2 * PAD
    state_shape = (variables, cells + 2 * HF, long_rows, lanes)
    source_shape = (variables, cells + 2 * HP, long_rows, lanes)
    corner = (corner_layout(variables)[1], lanes)

    inputs = (store, sample_times, harmonics, flow_state, prior_state)
    shapes = [store.shape, sample_times.shape, harmonics.shape, state_shape, flow_state.shape]
    store, times, active, state, prior, share, send = call(
        rebuild_shares,
        shapes + [(2,) + face, (1,) + face],
        *[pltpu.with_memory_space_constraint(a, pltpu.MemorySpace.HBM) for a in inputs],
        types=(F32, jnp.int32, jnp.int32, F32, F32, F32, F32),
        scratch=[pltpu.SemaphoreType.DMA((len(inputs) + 1,))],
        in_specs=[HBM] * len(inputs),
    )
    gathered, step = [lax.ppermute(send, "pitch", flip_pairs(slabs, 1))], 1
    source, first, second = call(
        functools.partial(pack_pitch, cells, rows), [source_shape, halo, halo], state, prior
    )
    first = lax.ppermute(first, "pitch", swap_pairs(slabs, 0))
    while 1 << step < slabs:
        [send] = call(
            functools.partial(join_shares, step), [(1 << step,) + face], share, *gathered
        )
        gathered.append(lax.ppermute(send, "pitch", flip_pairs(slabs, 1 << step)))
        step += 1
    second = lax.ppermute(second, "pitch", swap_pairs(slabs, 1))
    edge, corner_1 = call(
        functools.partial(pack_axial, cells, rows),
        [(edge_layout(variables, cells, 0)[1], lanes), corner],
        state,
        source,
    )
    edge = lax.ppermute(edge, "blk", swap_pairs(blocks, 1))
    corner_1 = lax.ppermute(corner_1, ("blk", "pitch"), diagonal_pairs(slabs, blocks, 0))
    ghost, corner_2 = call(
        functools.partial(join_ghosts, cells, rows, slabs),
        [(variables, 2, rows, lanes), corner],
        state,
        source,
        share,
        *gathered,
    )
    corner_2 = lax.ppermute(corner_2, ("blk", "pitch"), diagonal_pairs(slabs, blocks, 1))
    table, base, gain = call(
        prepare_close,
        [(2, orders - 1, 2 * part, lanes), (2,) + face, (2 * part, lanes)],
        store,
        times,
        active,
    )

    state, source, out = call(
        functools.partial(place_halos, cells, rows, slabs),
        [state_shape, source_shape, (edge_layout(variables, cells, HF)[1], lanes)],
        state,
        source,
        first,
        second,
        edge,
        corner_1,
        corner_2,
        ghost,
        gain,
        aliases={0: 0, 1: 1},
    )
    got = lax.ppermute(out, "blk", swap_pairs(blocks, 0))
    mid_shapes = [
        (variables, cells + 2 * HP, long_rows, lanes),
        (variables, cells + 2 * HP - 4, long_rows, lanes),
    ]
    flux_shape = (variables - 1, cells + 2 * HP + 2, long_rows, lanes)
    flux_scratch = [pltpu.VMEM(flux_shape, F32)] * 3
    sizes = (cells, rows, slabs, blocks)
    half_faces = (slabs // 2,) + face
    state, source, mid_1, mid_2, new, held, send = call(
        functools.partial(start_sections, *sizes),
        [state_shape, source_shape] + mid_shapes + [flow_state.shape, half_faces, half_faces],
        state,
        source,
        got,
        scratch=flux_scratch,
        aliases={0: 0, 1: 1},
        limit=12,
    )
    step = slabs.bit_length() - 2
    spread = []
    if step > 0:
        low = [(i, i + (1 << step)) for i in range(0, slabs, 2 << step)]
        pairs = low + [(slabs - 1 - i, slabs - 1 - j) for i, j in low]
        spread.append(lax.ppermute(send, "pitch", pairs))
    _, _, new = call(
        functools.partial(finish_sections, *sizes),
        mid_shapes + [flow_state.shape],
        state,
        source,
        mid_1,
        mid_2,
        new,
        scratch=flux_scratch,
        aliases={2: 0, 3: 1, 4: 2},
        limit=12,
    )
    while step > 0:
        half_faces = (held.shape[0] // 2,) + face
        held, send = call(
            functools.partial(pass_on, step), [half_faces, half_faces], held, spread[-1], new
        )
        step -= 1
        if step > 0:
            low = [(i, i + (1 << step)) for i in range(0, slabs, 2 << step)]
            pairs = low + [(slabs - 1 - i, slabs - 1 - j) for i, j in low]
            spread.append(lax.ppermute(send, "pitch", pairs))
    second_sample = lax.ppermute(send, "pitch", flip_pairs(slabs, 1))
    parts = 4
    pieces = [orders * i // parts for i in range(parts + 1)]
    half_store = pltpu.VMEM(store.shape[1:], F32)
    new_state, new_store = call(
        functools.partial(close_first, pieces),
        [flow_state.shape, store.shape],
        new,
        store,
        table,
        held,
        scratch=[half_store, pltpu.SemaphoreType.DMA((parts + 1,))],
        out_specs=[HBM, HBM],
    )
    new_store, new_ghosts = call(
        functools.partial(close_second, pieces),
        [store.shape, (2,) + face],
        new_store,
        store,
        table,
        base,
        gain,
        held,
        second_sample,
        scratch=[half_store, pltpu.VMEM((2,) + face, F32), pltpu.SemaphoreType.DMA((parts + 1,))],
        in_specs=[HBM] + [VMEM] * 6,
        out_specs=[HBM, HBM],
        aliases={0: 0},
    )
    return (
        new_state,
        new_store.reshape(fourier_store.shape),
        new_ghosts.reshape(2, signals, part, lanes),
    )


def solution(mesh):
    placed = (
        P(None, "pitch", "blk", None),
        P(None, "pitch", "blk", None),
        P(None, None, None, ("blk", "pitch"), None),
        P(None, ("blk", "pitch"), None),
        P(("blk", "pitch"), None),
    )
    return jax.shard_map(
        shards,
        mesh=mesh,
        in_specs=placed,
        out_specs=(
            P(None, "pitch", "blk", None),
            P(None, None, None, ("blk", "pitch"), None),
            P(None, None, ("blk", "pitch"), None),
        ),
        check_vma=False,
    )
```

```python
import functools
import math

import jax
import jax.numpy as jnp
from jax import lax
from jax.experimental import pallas as pl
from jax.experimental.pallas import tpu as pltpu
from jax.sharding import PartitionSpec as P


NT = 96

gamma_less = 0.4
diss_coeff = 0.03125
section_coefs = (1.0 / 3.0, 0.5, 1.0)
pseudo_step = 0.1
physical_step = 0.25
relax_rate = 0.125
lag_turns = 0.3
period = 2.0 * math.pi / NT
phase_lag = 2.0 * math.pi * lag_turns

HF = 2 * len(section_coefs)
HP = HF - 2
PAD = 8

F32 = jnp.float32
VMEM = pl.BlockSpec(memory_space=pltpu.VMEM)


HBM = pl.BlockSpec(memory_space=pltpu.MemorySpace.HBM)


def call(body, outs, *args, scratch=(), aliases=None, in_specs=None, out_specs=None, types=None, cost=0, limit=8):
    outs = [jax.ShapeDtypeStruct(shape, kind) for shape, kind in zip(outs, types or [F32] * len(outs))]
    moved = 4 * sum(math.prod(a.shape) for a in list(args) + outs)
    return pl.pallas_call(
        body,
        out_shape=outs,
        in_specs=in_specs or [VMEM] * len(args),
        out_specs=out_specs or [VMEM] * len(outs),
        scratch_shapes=list(scratch),
        input_output_aliases=aliases or {},
        compiler_params=pltpu.CompilerParams(vmem_limit_bytes=limit << 20),
        cost_estimate=pl.CostEstimate(flops=cost, bytes_accessed=moved, transcendentals=0),
    )(*args)


def is_even(axis):
    return lax.axis_index(axis) % 2 == 0


def source_of(flow, prior):
    return (2.0 / physical_step) * flow - (0.5 / physical_step) * prior


def pack_pitch(cells, rows, state_ref, prior_ref, source_ref, first_ref, second_ref):
    own_rows = slice(PAD, PAD + rows)
    even = is_even("pitch")
    source_ref[:, HP : HP + cells, own_rows] = source_of(
        state_ref[:, HF : HF + cells, own_rows], prior_ref[...]
    )
    for out_ref, top in ((first_ref, even), (second_ref, jnp.logical_not(even))):
        at = jnp.where(top, cells, HF)
        out_ref[:, :HF] = state_ref[:, pl.ds(at, HF), own_rows]
        at = jnp.where(top, cells, HP)
        out_ref[:, HF:] = source_ref[:, pl.ds(at, HP), own_rows]


def pack_axial(cells, rows, state_ref, source_ref, edge_1, edge_2, corner_ref):
    refs = (state_ref, source_ref)
    edges, _ = edge_layout(state_ref.shape[0], cells, 0)
    sides, _ = side_layout(state_ref.shape[0])
    top = is_even("pitch")

    def write(up):
        for v, which, depth, count, place in sides:
            width = (HF, HP)[which]
            plane = jnp.where(top, width + cells - depth, width + depth - 1)
            corner_ref[place : place + count] = refs[which][v, plane, edge_rows(rows, count, up)]
        for v, which, plane, count, place in edges:
            edge_1[place : place + count] = refs[which][v, plane, edge_rows(rows, count, not up)]
            edge_2[place : place + count] = refs[which][v, plane, edge_rows(rows, count, up)]

    pl.when(is_even("blk"))(lambda: write(False))
    pl.when(jnp.logical_not(is_even("blk")))(lambda: write(True))


def edge_rows(rows, count, up):
    return slice(PAD + rows - count, PAD + rows) if up else slice(PAD, PAD + count)


def halo_rows(rows, count, up):
    return slice(PAD + rows, PAD + rows + count) if up else slice(PAD - count, PAD)


def doubled(values):
    return jnp.concatenate([values, values], axis=0)


def share_sent(step):
    return jnp.where(lax.axis_index("pitch") % (2 << step) == 1 << step, 0, 1)


def rebuild_shares(*refs):
    store_hbm, times_hbm, active_hbm, flow_hbm, prior_hbm = refs[:5]
    store_ref, times_ref, active_ref, state_ref, prior_ref, share_ref, send_ref, sems = refs[5:]
    cells, rows = flow_hbm.shape[1:3]
    copies = [
        pltpu.make_async_copy(from_ref, to_ref, sems.at[i])
        for i, (from_ref, to_ref) in enumerate(
            (
                (times_hbm, times_ref),
                (active_hbm, active_ref),
                (store_hbm.at[0], store_ref.at[0]),
                (store_hbm.at[1], store_ref.at[1]),
                (flow_hbm, state_ref.at[:, pl.ds(HF, cells), pl.ds(PAD, rows)]),
                (prior_hbm, prior_ref),
            )
        )
    ]
    for copy in copies:
        copy.start()
    copies[0].wait()
    copies[1].wait()
    harm_count = (store_ref.shape[1] - 1) // 2
    signals = store_ref.shape[2]
    active = doubled(active_ref[...])
    for which in range(2):
        angle = doubled(times_ref[which]).astype(F32) * period
        angle = angle - phase_lag if which == 0 else angle + phase_lag
        cos_1, sin_1 = jnp.cos(angle), jnp.sin(angle)
        copies[2 + which].wait()
        cos_k, sin_k = cos_1, sin_1
        totals = [store_ref[which, 0, v] for v in range(signals)]
        for k in range(1, harm_count + 1):
            used = active >= k
            a, b = jnp.where(used, cos_k, 0.0), jnp.where(used, sin_k, 0.0)
            for v in range(signals):
                totals[v] = totals[v] + (
                    store_ref[which, k, v] * a + store_ref[which, harm_count + k, v] * b
                )
            cos_k, sin_k = cos_k * cos_1 - sin_k * sin_1, sin_k * cos_1 + cos_k * sin_1
        for v in range(signals):
            share_ref[which, v] = totals[v]
    send_ref[0] = share_ref[share_sent(0)]
    copies[4].wait()
    copies[5].wait()


def join_shares(step, share_ref, *refs):
    got_refs, out_ref = refs[:-1], refs[-1]
    out_ref[0] = share_ref[share_sent(step)]
    at = 1
    for got_ref in got_refs:
        out_ref[at : at + got_ref.shape[0]] = got_ref[...]
        at += got_ref.shape[0]


def radial_band(lanes):
    shape = (2 * lanes, lanes)
    source = lax.broadcasted_iota(jnp.int32, shape, 0)
    target = lax.broadcasted_iota(jnp.int32, shape, 1)
    fluxes = source >= lanes
    source = jnp.where(fluxes, source - lanes, source)

    def at(ahead):
        return source == jnp.clip(target + ahead, 0, lanes - 1)

    def entries(pairs):
        total = jnp.zeros(shape, F32)
        for ahead, value in pairs:
            total = total + jnp.where(at(ahead), value, 0.0)
        return total

    own = 1.5 / physical_step - 18.0 * diss_coeff
    state = [(1, 4.0), (-1, 4.0), (2, -1.0), (-2, -1.0), (0, own / diss_coeff)]
    state = entries([(ahead, diss_coeff * value) for ahead, value in state])
    return jnp.where(fluxes, entries([(1, 1.0), (-1, -1.0)]), state)


def prepare_close(store_ref, times_ref, active_ref, table_ref, base_ref, gain_ref, band_ref):
    band_ref[...] = radial_band(band_ref.shape[1]).astype(band_ref.dtype)
    harm_count = (store_ref.shape[1] - 1) // 2
    signals = store_ref.shape[2]
    active = doubled(active_ref[...])
    gain = jnp.full(active.shape, relax_rate, F32)
    for k in range(1, harm_count + 1):
        gain = gain + jnp.where(active >= k, 2.0 * relax_rate * math.cos(k * phase_lag), 0.0)
    gain_ref[...] = gain
    keep = 1.0 - relax_rate
    for which in range(2):
        angle = doubled(times_ref[which]).astype(F32) * period + period
        cos_1, sin_1 = jnp.cos(angle), jnp.sin(angle)
        cos_k, sin_k = cos_1, sin_1
        totals = [store_ref[which, 0, v] for v in range(signals)]
        turn = -phase_lag if which == 0 else phase_lag
        for k in range(1, harm_count + 1):
            table_ref[which, k - 1] = (2.0 * relax_rate) * cos_k
            table_ref[which, harm_count + k - 1] = (2.0 * relax_rate) * sin_k
            used = active >= k
            c, s = math.cos(k * turn), math.sin(k * turn)
            a = jnp.where(used, cos_k * c - sin_k * s, 0.0)
            b = jnp.where(used, sin_k * c + cos_k * s, 0.0)
            for v in range(signals):
                totals[v] = totals[v] + (
                    store_ref[which, k, v] * a + store_ref[which, harm_count + k, v] * b
                )
            cos_k, sin_k = cos_k * cos_1 - sin_k * sin_1, sin_k * cos_1 + cos_k * sin_1
        for v in range(signals):
            base_ref[which, v] = keep * totals[v]


def edge_layout(variables, cells, reach):
    parts, place = [], 0
    for v in range(variables):
        for which, width in ((0, HF), (1, HP)):
            out = min(reach, width - 1)
            for plane in range(-out, cells + out):
                count = width - max(0, -plane, plane - cells + 1)
                parts.append((v, which, plane + width, count, place))
                place += count
    return parts, -(-place // 8) * 8


def corner_layout(variables, cells):
    parts, place = [], 0
    for v, which, plane, count, _ in edge_layout(variables, cells, HF)[0]:
        if not 0 <= plane - (HF, HP)[which] < cells:
            parts.append((v, which, plane, count, place))
            place += count
    return parts, -(-place // 8) * 8


def side_layout(variables):
    parts, place = [], 0
    for v in range(variables):
        for which, width in ((0, HF), (1, HP)):
            for depth in range(1, width):
                parts.append((v, which, depth, width - depth, place))
                place += width - depth
    return parts, -(-place // 8) * 8


def halo_plane(cells, which, depth, upper):
    width = (HF, HP)[which]
    return jnp.where(upper, width + cells + depth - 1, width - depth)


def place_edges(cells, rows, slabs, blocks, *refs):
    edge_1, edge_2, band_ref = refs[2:5]
    state_ref, source_ref, mid_1 = refs[5:8]
    into = (state_ref, source_ref)
    edges, _ = edge_layout(state_ref.shape[0], cells, 0)

    def move(up):
        for v, which, plane, count, place in edges:
            into[which][v, plane, halo_rows(rows, count, not up)] = edge_1[place : place + count]
            into[which][v, plane, halo_rows(rows, count, up)] = edge_2[place : place + count]

    pl.when(is_even("blk"))(lambda: move(False))
    pl.when(jnp.logical_not(is_even("blk")))(lambda: move(True))
    block = Block(cells, rows, slabs, blocks, state_ref, source_ref, band_ref, refs[8:])
    block.clamp_ends(state_ref)
    block.advance(0, state_ref, mid_1, 2, cells - 2)


def place_halos(cells, rows, slabs, *refs):
    first_ref, second_ref, share_ref = refs[2:5]
    got_refs = refs[5:-4]
    state_ref, source_ref, out_ref, corner_ref = refs[-4:]
    refs = (state_ref, source_ref)
    pitch_at = lax.axis_index("pitch")
    even = is_even("pitch")
    blk_even = is_even("blk")
    variables = state_ref.shape[0]
    own_rows = slice(PAD, PAD + rows)
    for halo_ref, upper in ((first_ref, even), (second_ref, jnp.logical_not(even))):
        at = jnp.where(upper, HF + cells, 0)
        state_ref[:, pl.ds(at, HF), own_rows] = halo_ref[:, :HF]
        at = jnp.where(upper, HP + cells, 0)
        source_ref[:, pl.ds(at, HP), own_rows] = halo_ref[:, HF:]

    part = rows // slabs
    for end, plane in ((0, HF - 2), (1, HF + cells)):

        @pl.when(pitch_at == end * (slabs - 1))
        def _():
            pieces = [share_ref[end]]
            for got_ref in got_refs:
                pieces += [got_ref[i] for i in range(got_ref.shape[0])]
            for distance, piece in enumerate(pieces):
                at = PAD + part * (distance if end == 0 else slabs - 1 - distance)
                for layer in range(2):
                    state_ref[:, plane + layer, at : at + part] = piece[
                        :, layer * part : (layer + 1) * part
                    ]

    sides, _ = side_layout(variables)
    corners, _ = corner_layout(variables, cells)

    def move(up):
        for v, which, depth, count, place in sides:
            plane = halo_plane(cells, which, depth, jnp.logical_not(even))
            corner_ref[place : place + count] = refs[which][v, plane, edge_rows(rows, count, up)]
        for v, which, plane, count, place in corners:
            out_ref[place : place + count] = refs[which][v, plane, edge_rows(rows, count, not up)]

    pl.when(blk_even)(lambda: move(False))
    pl.when(jnp.logical_not(blk_even))(lambda: move(True))


class Block:
    def __init__(self, cells, rows, slabs, blocks, state_ref, source_ref, band_ref, flux_refs):
        self.cells, self.rows, self.slabs, self.blocks = cells, rows, slabs, blocks
        self.state_ref, self.source_ref, self.flux_refs = state_ref, source_ref, flux_refs
        self.band_ref = band_ref
        self.variables, _, _, self.lanes = state_ref.shape
        self.pitch_at = lax.axis_index("pitch")
        self.blk_at = lax.axis_index("blk")

    def clamp_ends(self, ref):
        rows = self.rows
        shape = (self.variables, ref.shape[1], 2, self.lanes)

        @pl.when(self.blk_at == 0)
        def _():
            ref[:, :, PAD - 2 : PAD] = jnp.broadcast_to(ref[:, :, PAD : PAD + 1], shape)

        @pl.when(self.blk_at == self.blocks - 1)
        def _():
            ref[:, :, PAD + rows : PAD + rows + 2] = jnp.broadcast_to(
                ref[:, :, PAD + rows - 1 : PAD + rows], shape
            )

    def keep_ghosts(self, ref, width):
        for end, at in ((0, 0), (self.slabs - 1, 2 + self.cells)):

            @pl.when(self.pitch_at == end)
            def _():
                ref[:, width - 2 + at : width + at] = self.state_ref[:, HF - 2 + at : HF + at]

    def advance(self, step, from_ref, to_ref, lo, hi):
        width = HF - 2 * step
        out_width = width - 2
        last = step == len(section_coefs) - 1
        scale = section_coefs[step] * pseudo_step
        count = -(-(self.rows + 2 * out_width) // 8) * 8
        row_at = PAD - out_width
        variables, lanes = self.variables, self.lanes
        pitch_ref, axial_ref, radial_ref = self.flux_refs

        def fluxes(plane):
            u = [from_ref[v, plane + width] for v in range(variables)]
            inverse = 1.0 / u[0]
            speed = [u[d] * inverse for d in (1, 2, 3)]
            pressure = gamma_less * (
                u[4] - 0.5 * (u[1] * speed[0] + u[2] * speed[1] + u[3] * speed[2])
            )
            half = 0.5 * pressure
            total = u[4] + pressure
            for d, flux_ref in enumerate((pitch_ref, axial_ref, radial_ref)):
                w = 0.5 * speed[d]
                for v in (1, 2, 3):
                    flux = u[v] * w
                    flux_ref[v - 1, plane + HP + 1] = flux + half if v == d + 1 else flux
                flux_ref[3, plane + HP + 1] = total * w

        def update(plane):
            at = slice(row_at, row_at + count)
            here = [from_ref[v, plane + width, at] for v in range(variables)]
            along = [0.5 * here[3]] + [radial_ref[v, plane + HP + 1, at] for v in range(variables - 1)]
            values = jnp.concatenate(
                [jnp.concatenate(pair, axis=1) for pair in zip(here, along)], axis=0
            )
            coarse = values.astype(jnp.bfloat16)
            fine = (values - coarse.astype(F32)).astype(jnp.bfloat16)
            band = self.band_ref[...]
            radial = jnp.dot(coarse, band, preferred_element_type=F32) + jnp.dot(
                fine, band, preferred_element_type=F32
            )
            for v in range(variables):

                def state(ahead, over):
                    return from_ref[v, plane + width + ahead, row_at + over : row_at + over + count]

                def change_of(ref, d, ahead, over):
                    def flux(sign):
                        at = row_at + sign * over
                        at = slice(at, at + count)
                        if v == 0:
                            return from_ref[d, plane + width + sign * ahead, at]
                        return ref[v - 1, plane + HP + 1 + sign * ahead, at]

                    return flux(1) - flux(-1)

                change = change_of(pitch_ref, 1, 1, 0) + change_of(axial_ref, 2, 0, 1)
                if v == 0:
                    change = 0.5 * change
                near = (state(1, 0) + state(-1, 0)) + (state(0, 1) + state(0, -1))
                far = (state(2, 0) + state(-2, 0)) + (state(0, 2) + state(0, -2))
                change = change + ((4.0 * diss_coeff) * near - diss_coeff * far)
                change = change + radial[v * count : (v + 1) * count]
                source = self.source_ref[v, plane + HP, at]
                flow = self.state_ref[v, plane + HF, at]
                to_at = row_at - PAD if last else row_at
                to_ref[v, plane + out_width, to_at : to_at + count] = flow + scale * (source - change)

        def pairs(body, start, stop):
            def both(index, carry):
                plane = start + 2 * index
                body(plane)
                body(plane + 1)
                return carry

            lax.fori_loop(0, (stop - start) // 2, both, 0)

        pairs(fluxes, lo - 1, hi + 1)
        pairs(update, lo, hi)
        if not last:
            self.clamp_ends(to_ref)


def start_sections(cells, rows, slabs, blocks, *refs):
    got_ref, corner_1, corner_2, band_ref = refs[2:6]
    state_ref, source_ref, mid_1, mid_2, new_ref, kept_ref, sent_ref = refs[7:14]
    flux_refs = refs[14:]
    block = Block(cells, rows, slabs, blocks, state_ref, source_ref, band_ref, flux_refs)
    variables = state_ref.shape[0]
    even = is_even("pitch")
    sides, _ = side_layout(variables)
    corners, _ = corner_layout(variables, cells)
    into = (state_ref, source_ref)

    def unpack(up):
        for v, which, plane, count, place in corners:
            into[which][v, plane, halo_rows(rows, count, not up)] = got_ref[place : place + count]
        for corner_ref, upper in ((corner_1, even), (corner_2, jnp.logical_not(even))):
            for v, which, depth, count, place in sides:
                plane = halo_plane(cells, which, depth, upper)
                into[which][v, plane, halo_rows(rows, count, up)] = corner_ref[place : place + count]

    pl.when(is_even("blk"))(lambda: unpack(False))
    pl.when(jnp.logical_not(is_even("blk")))(lambda: unpack(True))
    block.clamp_ends(state_ref)
    block.keep_ghosts(mid_1, HF - 2)
    block.keep_ghosts(mid_2, HF - 4)
    part = rows // slabs
    high = block.pitch_at == slabs - 1

    @pl.when((block.pitch_at == 0) | high)
    def _():
        for step, (from_ref, to_ref) in enumerate(
            ((state_ref, mid_1), (mid_1, mid_2), (mid_2, new_ref))
        ):
            planes = 2 if step == 0 else HF - 2 * step
            lo = jnp.where(high, cells - planes, 0)
            block.advance(step, from_ref, to_ref, lo, lo + planes)

    for end, plane in ((0, 0), (slabs - 1, cells - 2)):

        @pl.when(block.pitch_at == end)
        def _():
            for j in range(slabs):
                out_ref, i = (kept_ref, j) if 2 * j < slabs else (sent_ref, j - slabs // 2)
                at = (end ^ j) * part
                for layer in range(2):
                    out_ref[i, :, layer * part : (layer + 1) * part] = new_ref[
                        :, plane + layer, at : at + part
                    ]


def finish_sections(cells, rows, slabs, blocks, *refs):
    state_ref, source_ref, band_ref = refs[:3]
    mid_1, mid_2, new_ref = refs[6:9]
    block = Block(cells, rows, slabs, blocks, state_ref, source_ref, band_ref, refs[9:])
    low, high = block.pitch_at == 0, block.pitch_at == slabs - 1
    width = HF - 2
    pl.when(jnp.logical_not(low))(lambda: block.advance(0, state_ref, mid_1, -width, 2))
    pl.when(jnp.logical_not(high))(
        lambda: block.advance(0, state_ref, mid_1, cells - 2, cells + width)
    )
    for step, from_ref, to_ref in ((1, mid_1, mid_2), (2, mid_2, new_ref)):
        done = HF - 2 * step
        out_width = done - 2
        lo = jnp.where(low, done, -out_width)
        hi = jnp.where(high, cells - done, cells + out_width)
        block.advance(step, from_ref, to_ref, lo, hi)


def pass_on(step, held_ref, got_ref, after_ref, kept_ref, sent_ref):
    del after_ref
    at = lax.axis_index("pitch") % (2 << step)
    half = kept_ref.shape[0]
    got = (at == 1 << step) | (at == (1 << step) - 1)

    @pl.when(got)
    def _():
        kept_ref[...] = got_ref[:half]
        sent_ref[...] = got_ref[half:]

    @pl.when(jnp.logical_not(got))
    def _():
        kept_ref[...] = held_ref[:half]
        sent_ref[...] = held_ref[half:]


def refresh_half(pieces, which, sample_ref, store_ref, table_ref, fresh_ref, out_ref, send):
    keep = 1.0 - relax_rate
    sample = [sample_ref[0, v] for v in range(store_ref.shape[2])]
    for lo, hi in zip(pieces[:-1], pieces[1:]):
        for k in range(lo, hi):
            weight = relax_rate if k == 0 else table_ref[which, k - 1]
            for v, value in enumerate(sample):
                fresh_ref[k, v] = keep * store_ref[which, k, v] + weight * value
        window = pl.ds(lo, hi - lo)
        send(fresh_ref.at[window], out_ref.at[which, window])


def sender(sems):
    copies = []

    def send(from_ref, to_ref):
        copy = pltpu.make_async_copy(from_ref, to_ref, sems.at[len(copies)])
        copy.start()
        copies.append(copy)

    return copies, send


def close_first(pieces, new_ref, store_ref, table_ref, sample_ref, state_hbm, out_ref, fresh_ref, sems):
    copies, send = sender(sems)
    send(new_ref, state_hbm)
    which = 1 - lax.axis_index("pitch") % 2
    refresh_half(pieces, which, sample_ref, store_ref, table_ref, fresh_ref, out_ref, send)
    for copy in copies:
        copy.wait()


def close_second(pieces, *refs):
    store_ref, table_ref, base_ref, gain_ref, first_ref, second_ref = refs[1:7]
    out_ref, ghost_hbm, fresh_ref, ghost_ref, sems = refs[7:]
    copies, send = sender(sems)
    which = lax.axis_index("pitch") % 2
    gain = gain_ref[...]
    for at, sample_ref in ((1 - which, first_ref), (which, second_ref)):
        ghost_ref[at] = base_ref[at] + sample_ref[0] * gain[None]
    send(ghost_ref, ghost_hbm)
    refresh_half(pieces, which, second_ref, store_ref, table_ref, fresh_ref, out_ref, send)
    for copy in copies:
        copy.wait()


def swap_pairs(count, start):
    pairs = [(i, i + 1) for i in range(start, count - 1, 2)]
    return pairs + [(b, a) for a, b in pairs]


def flip_pairs(count, bits):
    return [(i, i ^ bits) for i in range(count)]


def diagonal_pairs(slabs, blocks, start):
    along = dict((i, i) for i in range(slabs))
    along.update(swap_pairs(slabs, start))
    return [
        (b * slabs + p, other * slabs + along[p])
        for b, other in swap_pairs(blocks, 1)
        for p in range(slabs)
    ]


def shards(flow_state, prior_state, fourier_store, sample_times, harmonics):
    slabs = lax.axis_size("pitch")
    blocks = lax.axis_size("blk")
    variables, cells, rows, lanes = flow_state.shape
    orders, signals, part = fourier_store.shape[1:4]
    store = fourier_store.reshape(2, orders, variables, 2 * part, lanes)
    halo = (variables, HF + HP, rows, lanes)
    face = (variables, 2 * part, lanes)
    long_rows = rows + 2 * PAD
    state_shape = (variables, cells + 2 * HF, long_rows, lanes)
    source_shape = (variables, cells + 2 * HP, long_rows, lanes)

    inputs = (store, sample_times, harmonics, flow_state, prior_state)
    shapes = [store.shape, sample_times.shape, harmonics.shape, state_shape, flow_state.shape]
    store, times, active, state, prior, share, send = call(
        rebuild_shares,
        shapes + [(2,) + face, (1,) + face],
        *[pltpu.with_memory_space_constraint(a, pltpu.MemorySpace.HBM) for a in inputs],
        types=(F32, jnp.int32, jnp.int32, F32, F32, F32, F32),
        scratch=[pltpu.SemaphoreType.DMA((len(inputs) + 1,))],
        in_specs=[HBM] * len(inputs),
    )
    gathered, step = [lax.ppermute(send, "pitch", flip_pairs(slabs, 1))], 1
    source, first, second = call(
        functools.partial(pack_pitch, cells, rows), [source_shape, halo, halo], state, prior
    )
    first = lax.ppermute(first, "pitch", swap_pairs(slabs, 0))
    second = lax.ppermute(second, "pitch", swap_pairs(slabs, 1))
    edge_shape = (edge_layout(variables, cells, 0)[1], lanes)
    side_shape = (side_layout(variables)[1], lanes)
    edge_1, edge_2, corner_1 = call(
        functools.partial(pack_axial, cells, rows),
        [edge_shape, edge_shape, side_shape],
        state,
        source,
    )
    edge_2 = lax.ppermute(edge_2, "blk", swap_pairs(blocks, 1))
    edge_1 = lax.ppermute(edge_1, "blk", swap_pairs(blocks, 0))
    corner_1 = lax.ppermute(corner_1, ("blk", "pitch"), diagonal_pairs(slabs, blocks, 0))
    while 1 << step < slabs:
        [send] = call(
            functools.partial(join_shares, step), [(1 << step,) + face], share, *gathered
        )
        gathered.append(lax.ppermute(send, "pitch", flip_pairs(slabs, 1 << step)))
        step += 1
    table, base, gain, band = call(
        prepare_close,
        [(2, orders - 1, 2 * part, lanes), (2,) + face, (2 * part, lanes), (2 * lanes, lanes)],
        store,
        times,
        active,
        types=[F32, F32, F32, jnp.bfloat16],
    )

    sizes = (cells, rows, slabs, blocks)
    mid_shapes = [
        (variables, cells + 2 * HP, long_rows, lanes),
        (variables, cells + 2 * HP - 4, long_rows, lanes),
    ]
    flux_shape = (variables - 1, cells + 2 * HP + 2, long_rows, lanes)
    flux_scratch = [pltpu.VMEM(flux_shape, F32)] * 3
    state, source, mid_1 = call(
        functools.partial(place_edges, *sizes),
        [state_shape, source_shape, mid_shapes[0]],
        state,
        source,
        edge_1,
        edge_2,
        band,
        scratch=flux_scratch,
        aliases={0: 0, 1: 1},
        limit=12,
    )
    state, source, out, corner_2 = call(
        functools.partial(place_halos, *sizes[:3]),
        [state_shape, source_shape, (corner_layout(variables, cells)[1], lanes), side_shape],
        state,
        source,
        first,
        second,
        share,
        *gathered,
        aliases={0: 0, 1: 1},
    )
    corner_2 = lax.ppermute(corner_2, "blk", swap_pairs(blocks, 1))
    got = lax.ppermute(out, "blk", swap_pairs(blocks, 0))
    half_faces = (slabs // 2,) + face
    state, source, mid_1, mid_2, new, held, send = call(
        functools.partial(start_sections, *sizes),
        [state_shape, source_shape]
        + mid_shapes
        + [flow_state.shape, half_faces, half_faces],
        state,
        source,
        got,
        corner_1,
        corner_2,
        band,
        mid_1,
        scratch=flux_scratch,
        aliases={0: 0, 1: 1, 6: 2},
        limit=12,
    )
    step = slabs.bit_length() - 2
    spread = []
    if step > 0:
        low = [(i, i + (1 << step)) for i in range(0, slabs, 2 << step)]
        pairs = low + [(slabs - 1 - i, slabs - 1 - j) for i, j in low]
        spread.append(lax.ppermute(send, "pitch", pairs))
    _, _, new = call(
        functools.partial(finish_sections, *sizes),
        mid_shapes + [flow_state.shape],
        state,
        source,
        band,
        mid_1,
        mid_2,
        new,
        scratch=flux_scratch,
        aliases={3: 0, 4: 1, 5: 2},
        limit=12,
    )
    while step > 0:
        half_faces = (held.shape[0] // 2,) + face
        held, send = call(
            functools.partial(pass_on, step), [half_faces, half_faces], held, spread[-1], new
        )
        step -= 1
        if step > 0:
            low = [(i, i + (1 << step)) for i in range(0, slabs, 2 << step)]
            pairs = low + [(slabs - 1 - i, slabs - 1 - j) for i, j in low]
            spread.append(lax.ppermute(send, "pitch", pairs))
    second_sample = lax.ppermute(send, "pitch", flip_pairs(slabs, 1))
    parts = 4
    pieces = [orders * i // parts for i in range(parts + 1)]
    half_store = pltpu.VMEM(store.shape[1:], F32)
    new_state, new_store = call(
        functools.partial(close_first, pieces),
        [flow_state.shape, store.shape],
        new,
        store,
        table,
        held,
        scratch=[half_store, pltpu.SemaphoreType.DMA((parts + 1,))],
        out_specs=[HBM, HBM],
    )
    new_store, new_ghosts = call(
        functools.partial(close_second, pieces),
        [store.shape, (2,) + face],
        new_store,
        store,
        table,
        base,
        gain,
        held,
        second_sample,
        scratch=[half_store, pltpu.VMEM((2,) + face, F32), pltpu.SemaphoreType.DMA((parts + 1,))],
        in_specs=[HBM] + [VMEM] * 6,
        out_specs=[HBM, HBM],
        aliases={0: 0},
    )
    return (
        new_state,
        new_store.reshape(fourier_store.shape),
        new_ghosts.reshape(2, signals, part, lanes),
    )


def solution(mesh):
    placed = (
        P(None, "pitch", "blk", None),
        P(None, "pitch", "blk", None),
        P(None, None, None, ("blk", "pitch"), None),
        P(None, ("blk", "pitch"), None),
        P(("blk", "pitch"), None),
    )
    return jax.shard_map(
        shards,
        mesh=mesh,
        in_specs=placed,
        out_specs=(
            P(None, "pitch", "blk", None),
            P(None, None, None, ("blk", "pitch"), None),
            P(None, None, ("blk", "pitch"), None),
        ),
        check_vma=False,
    )
```

```python
import functools
import math

import jax
import jax.numpy as jnp
from jax import lax
from jax.experimental import pallas as pl
from jax.experimental.pallas import tpu as pltpu
from jax.sharding import PartitionSpec as P


NT = 96

gamma_less = 0.4
diss_coeff = 0.03125
section_coefs = (1.0 / 3.0, 0.5, 1.0)
pseudo_step = 0.1
physical_step = 0.25
relax_rate = 0.125
lag_turns = 0.3
period = 2.0 * math.pi / NT
phase_lag = 2.0 * math.pi * lag_turns

HF = 2 * len(section_coefs)
HP = HF - 2
PAD = 8

F32 = jnp.float32
VMEM = pl.BlockSpec(memory_space=pltpu.VMEM)


HBM = pl.BlockSpec(memory_space=pltpu.MemorySpace.HBM)


def call(body, outs, *args, scratch=(), aliases=None, in_specs=None, out_specs=None, types=None, cost=0, limit=8):
    outs = [jax.ShapeDtypeStruct(shape, kind) for shape, kind in zip(outs, types or [F32] * len(outs))]
    moved = 4 * sum(math.prod(a.shape) for a in list(args) + outs)
    return pl.pallas_call(
        body,
        out_shape=outs,
        in_specs=in_specs or [VMEM] * len(args),
        out_specs=out_specs or [VMEM] * len(outs),
        scratch_shapes=list(scratch),
        input_output_aliases=aliases or {},
        compiler_params=pltpu.CompilerParams(vmem_limit_bytes=limit << 20),
        cost_estimate=pl.CostEstimate(flops=cost, bytes_accessed=moved, transcendentals=0),
    )(*args)


def is_even(axis):
    return lax.axis_index(axis) % 2 == 0


def source_of(flow, prior):
    return (2.0 / physical_step) * flow - (0.5 / physical_step) * prior


def pack_pitch(cells, rows, state_ref, prior_ref, source_ref, first_ref, second_ref):
    own_rows = slice(PAD, PAD + rows)
    even = is_even("pitch")
    source_ref[:, HP : HP + cells, own_rows] = source_of(
        state_ref[:, HF : HF + cells, own_rows], prior_ref[...]
    )
    for out_ref, top in ((first_ref, even), (second_ref, jnp.logical_not(even))):
        at = jnp.where(top, cells, HF)
        out_ref[:, :HF] = state_ref[:, pl.ds(at, HF), own_rows]
        at = jnp.where(top, cells, HP)
        out_ref[:, HF:] = source_ref[:, pl.ds(at, HP), own_rows]


def pack_axial(cells, rows, state_ref, source_ref, edge_1, edge_2, corner_1, corner_2):
    refs = (state_ref, source_ref)
    edges, _ = edge_layout(state_ref.shape[0], cells, 0)
    sides, _ = side_layout(state_ref.shape[0])
    even = is_even("pitch")

    def write(up):
        for corner_ref, top in ((corner_1, even), (corner_2, jnp.logical_not(even))):
            for v, which, depth, count, place in sides:
                width = (HF, HP)[which]
                plane = jnp.where(top, width + cells - depth, width + depth - 1)
                corner_ref[place : place + count] = refs[which][v, plane, edge_rows(rows, count, up)]
        for v, which, plane, count, place in edges:
            edge_1[place : place + count] = refs[which][v, plane, edge_rows(rows, count, not up)]
            edge_2[place : place + count] = refs[which][v, plane, edge_rows(rows, count, up)]

    pl.when(is_even("blk"))(lambda: write(False))
    pl.when(jnp.logical_not(is_even("blk")))(lambda: write(True))


def edge_rows(rows, count, up):
    return slice(PAD + rows - count, PAD + rows) if up else slice(PAD, PAD + count)


def halo_rows(rows, count, up):
    return slice(PAD + rows, PAD + rows + count) if up else slice(PAD - count, PAD)


def doubled(values):
    return jnp.concatenate([values, values], axis=0)


def share_sent(step):
    return jnp.where(lax.axis_index("pitch") % (2 << step) == 1 << step, 0, 1)


def rebuild_shares(*refs):
    store_hbm, times_hbm, active_hbm, flow_hbm, prior_hbm = refs[:5]
    store_ref, times_ref, active_ref, state_ref, prior_ref, share_ref, send_ref, sems = refs[5:]
    cells, rows = flow_hbm.shape[1:3]
    copies = [
        pltpu.make_async_copy(from_ref, to_ref, sems.at[i])
        for i, (from_ref, to_ref) in enumerate(
            (
                (times_hbm, times_ref),
                (active_hbm, active_ref),
                (store_hbm.at[0], store_ref.at[0]),
                (store_hbm.at[1], store_ref.at[1]),
                (flow_hbm, state_ref.at[:, pl.ds(HF, cells), pl.ds(PAD, rows)]),
                (prior_hbm, prior_ref),
            )
        )
    ]
    for copy in copies:
        copy.start()
    copies[0].wait()
    copies[1].wait()
    harm_count = (store_ref.shape[1] - 1) // 2
    signals = store_ref.shape[2]
    active = doubled(active_ref[...])
    for which in range(2):
        angle = doubled(times_ref[which]).astype(F32) * period
        angle = angle - phase_lag if which == 0 else angle + phase_lag
        cos_1, sin_1 = jnp.cos(angle), jnp.sin(angle)
        copies[2 + which].wait()
        cos_k, sin_k = cos_1, sin_1
        totals = [store_ref[which, 0, v] for v in range(signals)]
        for k in range(1, harm_count + 1):
            used = active >= k
            a, b = jnp.where(used, cos_k, 0.0), jnp.where(used, sin_k, 0.0)
            for v in range(signals):
                totals[v] = totals[v] + (
                    store_ref[which, k, v] * a + store_ref[which, harm_count + k, v] * b
                )
            cos_k, sin_k = cos_k * cos_1 - sin_k * sin_1, sin_k * cos_1 + cos_k * sin_1
        for v in range(signals):
            share_ref[which, v] = totals[v]
    send_ref[0] = share_ref[share_sent(0)]
    copies[4].wait()
    copies[5].wait()


def join_shares(step, share_ref, *refs):
    got_refs, out_ref = refs[:-1], refs[-1]
    out_ref[0] = share_ref[share_sent(step)]
    at = 1
    for got_ref in got_refs:
        out_ref[at : at + got_ref.shape[0]] = got_ref[...]
        at += got_ref.shape[0]


def radial_band(lanes):
    shape = (2 * lanes, lanes)
    source = lax.broadcasted_iota(jnp.int32, shape, 0)
    target = lax.broadcasted_iota(jnp.int32, shape, 1)
    fluxes = source >= lanes
    source = jnp.where(fluxes, source - lanes, source)

    def at(ahead):
        return source == jnp.clip(target + ahead, 0, lanes - 1)

    def entries(pairs):
        total = jnp.zeros(shape, F32)
        for ahead, value in pairs:
            total = total + jnp.where(at(ahead), value, 0.0)
        return total

    own = 1.5 / physical_step - 18.0 * diss_coeff
    state = [(1, 4.0), (-1, 4.0), (2, -1.0), (-2, -1.0), (0, own / diss_coeff)]
    state = entries([(ahead, diss_coeff * value) for ahead, value in state])
    return jnp.where(fluxes, entries([(1, 1.0), (-1, -1.0)]), state)


def prepare_close(store_ref, times_ref, active_ref, table_ref, base_ref, gain_ref, band_ref):
    band_ref[...] = radial_band(band_ref.shape[1]).astype(band_ref.dtype)
    harm_count = (store_ref.shape[1] - 1) // 2
    signals = store_ref.shape[2]
    active = doubled(active_ref[...])
    gain = jnp.full(active.shape, relax_rate, F32)
    for k in range(1, harm_count + 1):
        gain = gain + jnp.where(active >= k, 2.0 * relax_rate * math.cos(k * phase_lag), 0.0)
    gain_ref[...] = gain
    keep = 1.0 - relax_rate
    for which in range(2):
        angle = doubled(times_ref[which]).astype(F32) * period + period
        cos_1, sin_1 = jnp.cos(angle), jnp.sin(angle)
        cos_k, sin_k = cos_1, sin_1
        totals = [store_ref[which, 0, v] for v in range(signals)]
        turn = -phase_lag if which == 0 else phase_lag
        for k in range(1, harm_count + 1):
            table_ref[which, k - 1] = (2.0 * relax_rate) * cos_k
            table_ref[which, harm_count + k - 1] = (2.0 * relax_rate) * sin_k
            used = active >= k
            c, s = math.cos(k * turn), math.sin(k * turn)
            a = jnp.where(used, cos_k * c - sin_k * s, 0.0)
            b = jnp.where(used, sin_k * c + cos_k * s, 0.0)
            for v in range(signals):
                totals[v] = totals[v] + (
                    store_ref[which, k, v] * a + store_ref[which, harm_count + k, v] * b
                )
            cos_k, sin_k = cos_k * cos_1 - sin_k * sin_1, sin_k * cos_1 + cos_k * sin_1
        for v in range(signals):
            base_ref[which, v] = keep * totals[v]


def edge_layout(variables, cells, reach):
    parts, place = [], 0
    for v in range(variables):
        for which, width in ((0, HF), (1, HP)):
            out = min(reach, width - 1)
            for plane in range(-out, cells + out):
                count = width - max(0, -plane, plane - cells + 1)
                parts.append((v, which, plane + width, count, place))
                place += count
    return parts, -(-place // 8) * 8


def corner_layout(variables, cells):
    parts, place = [], 0
    for v, which, plane, count, _ in edge_layout(variables, cells, HF)[0]:
        if not 0 <= plane - (HF, HP)[which] < cells:
            parts.append((v, which, plane, count, place))
            place += count
    return parts, -(-place // 8) * 8


def side_layout(variables):
    parts, place = [], 0
    for v in range(variables):
        for which, width in ((0, HF), (1, HP)):
            for depth in range(1, width):
                parts.append((v, which, depth, width - depth, place))
                place += width - depth
    return parts, -(-place // 8) * 8


def halo_plane(cells, which, depth, upper):
    width = (HF, HP)[which]
    return jnp.where(upper, width + cells + depth - 1, width - depth)


def place_edges(cells, rows, slabs, blocks, *refs):
    edge_1, edge_2, band_ref = refs[2:5]
    state_ref, source_ref, mid_1 = refs[6:9]
    into = (state_ref, source_ref)
    edges, _ = edge_layout(state_ref.shape[0], cells, 0)

    def move(up):
        for v, which, plane, count, place in edges:
            into[which][v, plane, halo_rows(rows, count, not up)] = edge_1[place : place + count]
            into[which][v, plane, halo_rows(rows, count, up)] = edge_2[place : place + count]

    pl.when(is_even("blk"))(lambda: move(False))
    pl.when(jnp.logical_not(is_even("blk")))(lambda: move(True))
    block = Block(cells, rows, slabs, blocks, state_ref, source_ref, band_ref, refs[9:])
    block.clamp_ends(state_ref)
    block.advance(0, state_ref, mid_1, 2, cells - 2)


def join_ghosts(rows, slabs, share_ref, after_ref, *refs):
    del after_ref
    got_refs, (ghost_ref, send_ref) = refs[:-2], refs[-2:]
    part = rows // slabs
    variables = ghost_ref.shape[0]
    for end in range(2):

        @pl.when(lax.axis_index("pitch") == end * (slabs - 1))
        def _():
            pieces = [share_ref[end]]
            for got_ref in got_refs:
                pieces += [got_ref[i] for i in range(got_ref.shape[0])]
            for distance, piece in enumerate(pieces):
                at = part * (distance if end == 0 else slabs - 1 - distance)
                for layer in range(2):
                    ghost_ref[:, layer, at : at + part] = piece[:, layer * part : (layer + 1) * part]

    def write(at):
        for v in range(variables):
            for layer in range(2):
                place = (2 * v + layer) * HP
                send_ref[place : place + HP] = ghost_ref[v, layer, at : at + HP]

    pl.when(is_even("blk"))(lambda: write(0))
    pl.when(jnp.logical_not(is_even("blk")))(lambda: write(rows - HP))


def ghost_planes(cells, end):
    return HF + cells if end else HF - 2


def place_halos(cells, rows, slabs, *refs):
    first_ref, second_ref, ghost_ref = refs[2:5]
    state_ref, source_ref, out_ref = refs[-3:]
    refs = (state_ref, source_ref)
    even = is_even("pitch")
    variables = state_ref.shape[0]
    own_rows = slice(PAD, PAD + rows)
    for halo_ref, upper in ((first_ref, even), (second_ref, jnp.logical_not(even))):
        at = jnp.where(upper, HF + cells, 0)
        state_ref[:, pl.ds(at, HF), own_rows] = halo_ref[:, :HF]
        at = jnp.where(upper, HP + cells, 0)
        source_ref[:, pl.ds(at, HP), own_rows] = halo_ref[:, HF:]
    for end in range(2):

        @pl.when(lax.axis_index("pitch") == end * (slabs - 1))
        def _():
            plane = ghost_planes(cells, end)
            state_ref[:, plane : plane + 2, own_rows] = ghost_ref[...]

    corners, _ = corner_layout(variables, cells)

    def move(up):
        for v, which, plane, count, place in corners:
            out_ref[place : place + count] = refs[which][v, plane, edge_rows(rows, count, up)]

    pl.when(is_even("blk"))(lambda: move(True))
    pl.when(jnp.logical_not(is_even("blk")))(lambda: move(False))


class Block:
    def __init__(self, cells, rows, slabs, blocks, state_ref, source_ref, band_ref, flux_refs):
        self.cells, self.rows, self.slabs, self.blocks = cells, rows, slabs, blocks
        self.state_ref, self.source_ref, self.flux_refs = state_ref, source_ref, flux_refs
        self.band_ref = band_ref
        self.variables, _, _, self.lanes = state_ref.shape
        self.pitch_at = lax.axis_index("pitch")
        self.blk_at = lax.axis_index("blk")

    def clamp_ends(self, ref):
        rows = self.rows
        shape = (self.variables, ref.shape[1], 2, self.lanes)

        @pl.when(self.blk_at == 0)
        def _():
            ref[:, :, PAD - 2 : PAD] = jnp.broadcast_to(ref[:, :, PAD : PAD + 1], shape)

        @pl.when(self.blk_at == self.blocks - 1)
        def _():
            ref[:, :, PAD + rows : PAD + rows + 2] = jnp.broadcast_to(
                ref[:, :, PAD + rows - 1 : PAD + rows], shape
            )

    def keep_ghosts(self, ref, width):
        for end, at in ((0, 0), (self.slabs - 1, 2 + self.cells)):

            @pl.when(self.pitch_at == end)
            def _():
                ref[:, width - 2 + at : width + at] = self.state_ref[:, HF - 2 + at : HF + at]

    def advance(self, step, from_ref, to_ref, lo, hi):
        width = HF - 2 * step
        out_width = width - 2
        last = step == len(section_coefs) - 1
        scale = section_coefs[step] * pseudo_step
        count = -(-(self.rows + 2 * out_width) // 8) * 8
        row_at = PAD - out_width
        variables, lanes = self.variables, self.lanes
        pitch_ref, axial_ref, radial_ref = self.flux_refs

        def fluxes(plane):
            u = [from_ref[v, plane + width] for v in range(variables)]
            inverse = 1.0 / u[0]
            speed = [u[d] * inverse for d in (1, 2, 3)]
            pressure = gamma_less * (
                u[4] - 0.5 * (u[1] * speed[0] + u[2] * speed[1] + u[3] * speed[2])
            )
            half = 0.5 * pressure
            total = u[4] + pressure
            for d, flux_ref in enumerate((pitch_ref, axial_ref, radial_ref)):
                w = 0.5 * speed[d]
                for v in (1, 2, 3):
                    flux = u[v] * w
                    flux_ref[v - 1, plane + HP + 1] = flux + half if v == d + 1 else flux
                flux_ref[3, plane + HP + 1] = total * w

        def update(plane):
            at = slice(row_at, row_at + count)
            here = [from_ref[v, plane + width, at] for v in range(variables)]
            along = [0.5 * here[3]] + [radial_ref[v, plane + HP + 1, at] for v in range(variables - 1)]
            values = jnp.concatenate(
                [jnp.concatenate(pair, axis=1) for pair in zip(here, along)], axis=0
            )
            coarse = values.astype(jnp.bfloat16)
            fine = (values - coarse.astype(F32)).astype(jnp.bfloat16)
            band = self.band_ref[...]
            radial = jnp.dot(coarse, band, preferred_element_type=F32) + jnp.dot(
                fine, band, preferred_element_type=F32
            )
            for v in range(variables):

                def state(ahead, over):
                    return from_ref[v, plane + width + ahead, row_at + over : row_at + over + count]

                def change_of(ref, d, ahead, over):
                    def flux(sign):
                        at = row_at + sign * over
                        at = slice(at, at + count)
                        if v == 0:
                            return from_ref[d, plane + width + sign * ahead, at]
                        return ref[v - 1, plane + HP + 1 + sign * ahead, at]

                    return flux(1) - flux(-1)

                change = change_of(pitch_ref, 1, 1, 0) + change_of(axial_ref, 2, 0, 1)
                if v == 0:
                    change = 0.5 * change
                near = (state(1, 0) + state(-1, 0)) + (state(0, 1) + state(0, -1))
                far = (state(2, 0) + state(-2, 0)) + (state(0, 2) + state(0, -2))
                change = change + ((4.0 * diss_coeff) * near - diss_coeff * far)
                change = change + radial[v * count : (v + 1) * count]
                source = self.source_ref[v, plane + HP, at]
                flow = self.state_ref[v, plane + HF, at]
                to_at = row_at - PAD if last else row_at
                to_ref[v, plane + out_width, to_at : to_at + count] = flow + scale * (source - change)

        def pairs(body, start, stop):
            def both(index, carry):
                plane = start + 2 * index
                body(plane)
                body(plane + 1)
                return carry

            lax.fori_loop(0, (stop - start) // 2, both, 0)

        pairs(fluxes, lo - 1, hi + 1)
        pairs(update, lo, hi)
        if not last:
            self.clamp_ends(to_ref)


def start_sections(cells, rows, slabs, blocks, *refs):
    got_ref, corner_1, corner_2, beyond_ref, band_ref = refs[2:7]
    state_ref, source_ref, mid_1, mid_2, new_ref, kept_ref, sent_ref = refs[8:15]
    flux_refs = refs[15:]
    block = Block(cells, rows, slabs, blocks, state_ref, source_ref, band_ref, flux_refs)
    variables = state_ref.shape[0]
    even = is_even("pitch")
    sides, _ = side_layout(variables)
    corners, _ = corner_layout(variables, cells)
    into = (state_ref, source_ref)

    def unpack(up):
        for v, which, plane, count, place in corners:
            into[which][v, plane, halo_rows(rows, count, not up)] = got_ref[place : place + count]
        for corner_ref, upper in ((corner_1, even), (corner_2, jnp.logical_not(even))):
            for v, which, depth, count, place in sides:
                plane = halo_plane(cells, which, depth, upper)
                into[which][v, plane, halo_rows(rows, count, up)] = corner_ref[place : place + count]
        for end in range(2):

            @pl.when(block.pitch_at == end * (slabs - 1))
            def _():
                for v in range(variables):
                    for layer in range(2):
                        place = (2 * v + layer) * HP
                        plane = ghost_planes(cells, end) + layer
                        state_ref[v, plane, halo_rows(rows, HP, up)] = beyond_ref[place : place + HP]

    pl.when(is_even("blk"))(lambda: unpack(False))
    pl.when(jnp.logical_not(is_even("blk")))(lambda: unpack(True))
    block.clamp_ends(state_ref)
    block.keep_ghosts(mid_1, HF - 2)
    block.keep_ghosts(mid_2, HF - 4)
    part = rows // slabs
    high = block.pitch_at == slabs - 1

    @pl.when((block.pitch_at == 0) | high)
    def _():
        for step, (from_ref, to_ref) in enumerate(
            ((state_ref, mid_1), (mid_1, mid_2), (mid_2, new_ref))
        ):
            planes = 2 if step == 0 else HF - 2 * step
            lo = jnp.where(high, cells - planes, 0)
            block.advance(step, from_ref, to_ref, lo, lo + planes)

    for end, plane in ((0, 0), (slabs - 1, cells - 2)):

        @pl.when(block.pitch_at == end)
        def _():
            for j in range(slabs):
                out_ref, i = (kept_ref, j) if 2 * j < slabs else (sent_ref, j - slabs // 2)
                at = (end ^ j) * part
                for layer in range(2):
                    out_ref[i, :, layer * part : (layer + 1) * part] = new_ref[
                        :, plane + layer, at : at + part
                    ]


def finish_sections(cells, rows, slabs, blocks, *refs):
    state_ref, source_ref, band_ref = refs[:3]
    mid_1, mid_2, new_ref = refs[6:9]
    block = Block(cells, rows, slabs, blocks, state_ref, source_ref, band_ref, refs[9:])
    low, high = block.pitch_at == 0, block.pitch_at == slabs - 1
    width = HF - 2
    pl.when(jnp.logical_not(low))(lambda: block.advance(0, state_ref, mid_1, -width, 2))
    pl.when(jnp.logical_not(high))(
        lambda: block.advance(0, state_ref, mid_1, cells - 2, cells + width)
    )
    for step, from_ref, to_ref in ((1, mid_1, mid_2), (2, mid_2, new_ref)):
        done = HF - 2 * step
        out_width = done - 2
        lo = jnp.where(low, done, -out_width)
        hi = jnp.where(high, cells - done, cells + out_width)
        block.advance(step, from_ref, to_ref, lo, hi)


def pass_on(step, held_ref, got_ref, after_ref, kept_ref, sent_ref):
    del after_ref
    at = lax.axis_index("pitch") % (2 << step)
    half = kept_ref.shape[0]
    got = (at == 1 << step) | (at == (1 << step) - 1)

    @pl.when(got)
    def _():
        kept_ref[...] = got_ref[:half]
        sent_ref[...] = got_ref[half:]

    @pl.when(jnp.logical_not(got))
    def _():
        kept_ref[...] = held_ref[:half]
        sent_ref[...] = held_ref[half:]


def refresh_half(pieces, which, sample_ref, store_ref, table_ref, fresh_ref, out_ref, send):
    keep = 1.0 - relax_rate
    sample = [sample_ref[0, v] for v in range(store_ref.shape[2])]
    for lo, hi in zip(pieces[:-1], pieces[1:]):
        for k in range(lo, hi):
            weight = relax_rate if k == 0 else table_ref[which, k - 1]
            for v, value in enumerate(sample):
                fresh_ref[k, v] = keep * store_ref[which, k, v] + weight * value
        window = pl.ds(lo, hi - lo)
        send(fresh_ref.at[window], out_ref.at[which, window])


def sender(sems):
    copies = []

    def send(from_ref, to_ref):
        copy = pltpu.make_async_copy(from_ref, to_ref, sems.at[len(copies)])
        copy.start()
        copies.append(copy)

    return copies, send


def close_first(pieces, new_ref, store_ref, table_ref, sample_ref, state_hbm, out_ref, fresh_ref, sems):
    copies, send = sender(sems)
    send(new_ref, state_hbm)
    which = 1 - lax.axis_index("pitch") % 2
    refresh_half(pieces, which, sample_ref, store_ref, table_ref, fresh_ref, out_ref, send)
    for copy in copies:
        copy.wait()


def close_second(pieces, *refs):
    store_ref, table_ref, base_ref, gain_ref, first_ref, second_ref = refs[1:7]
    out_ref, ghost_hbm, fresh_ref, ghost_ref, sems = refs[7:]
    copies, send = sender(sems)
    which = lax.axis_index("pitch") % 2
    gain = gain_ref[...]
    for at, sample_ref in ((1 - which, first_ref), (which, second_ref)):
        ghost_ref[at] = base_ref[at] + sample_ref[0] * gain[None]
    send(ghost_ref, ghost_hbm)
    refresh_half(pieces, which, second_ref, store_ref, table_ref, fresh_ref, out_ref, send)
    for copy in copies:
        copy.wait()


def swap_pairs(count, start):
    pairs = [(i, i + 1) for i in range(start, count - 1, 2)]
    return pairs + [(b, a) for a, b in pairs]


def flip_pairs(count, bits):
    return [(i, i ^ bits) for i in range(count)]


def diagonal_pairs(slabs, blocks, start):
    return [
        (b * slabs + p, other * slabs + q)
        for b, other in swap_pairs(blocks, 1)
        for p, q in swap_pairs(slabs, start)
    ]


def end_pairs(slabs, blocks):
    return [
        (b * slabs + p, other * slabs + p)
        for b, other in swap_pairs(blocks, 1)
        for p in (0, slabs - 1)
    ]


def shards(flow_state, prior_state, fourier_store, sample_times, harmonics):
    slabs = lax.axis_size("pitch")
    blocks = lax.axis_size("blk")
    variables, cells, rows, lanes = flow_state.shape
    orders, signals, part = fourier_store.shape[1:4]
    store = fourier_store.reshape(2, orders, variables, 2 * part, lanes)
    halo = (variables, HF + HP, rows, lanes)
    face = (variables, 2 * part, lanes)
    long_rows = rows + 2 * PAD
    state_shape = (variables, cells + 2 * HF, long_rows, lanes)
    source_shape = (variables, cells + 2 * HP, long_rows, lanes)

    inputs = (store, sample_times, harmonics, flow_state, prior_state)
    shapes = [store.shape, sample_times.shape, harmonics.shape, state_shape, flow_state.shape]
    store, times, active, state, prior, share, send = call(
        rebuild_shares,
        shapes + [(2,) + face, (1,) + face],
        *[pltpu.with_memory_space_constraint(a, pltpu.MemorySpace.HBM) for a in inputs],
        types=(F32, jnp.int32, jnp.int32, F32, F32, F32, F32),
        scratch=[pltpu.SemaphoreType.DMA((len(inputs) + 1,))],
        in_specs=[HBM] * len(inputs),
    )
    gathered, step = [lax.ppermute(send, "pitch", flip_pairs(slabs, 1))], 1
    source, first, second = call(
        functools.partial(pack_pitch, cells, rows), [source_shape, halo, halo], state, prior
    )
    first = lax.ppermute(first, "pitch", swap_pairs(slabs, 0))
    second = lax.ppermute(second, "pitch", swap_pairs(slabs, 1))
    edge_shape = (edge_layout(variables, cells, 0)[1], lanes)
    side_shape = (side_layout(variables)[1], lanes)
    edge_1, edge_2, corner_1, corner_2 = call(
        functools.partial(pack_axial, cells, rows),
        [edge_shape, edge_shape, side_shape, side_shape],
        state,
        source,
    )
    edge_2 = lax.ppermute(edge_2, "blk", swap_pairs(blocks, 1))
    edge_1 = lax.ppermute(edge_1, "blk", swap_pairs(blocks, 0))
    both = ("blk", "pitch")
    corner_1 = lax.ppermute(corner_1, both, diagonal_pairs(slabs, blocks, 0))
    corner_2 = lax.ppermute(corner_2, both, diagonal_pairs(slabs, blocks, 1))
    while 1 << step < slabs:
        [send] = call(
            functools.partial(join_shares, step), [(1 << step,) + face], share, *gathered
        )
        gathered.append(lax.ppermute(send, "pitch", flip_pairs(slabs, 1 << step)))
        step += 1
    table, base, gain, band = call(
        prepare_close,
        [(2, orders - 1, 2 * part, lanes), (2,) + face, (2 * part, lanes), (2 * lanes, lanes)],
        store,
        times,
        active,
        types=[F32, F32, F32, jnp.bfloat16],
    )

    sizes = (cells, rows, slabs, blocks)
    mid_shapes = [
        (variables, cells + 2 * HP, long_rows, lanes),
        (variables, cells + 2 * HP - 4, long_rows, lanes),
    ]
    flux_shape = (variables - 1, cells + 2 * HP + 2, long_rows, lanes)
    flux_scratch = [pltpu.VMEM(flux_shape, F32)] * 3
    ghost, beyond = call(
        functools.partial(join_ghosts, rows, slabs),
        [(variables, 2, rows, lanes), (2 * variables * HP, lanes)],
        share,
        edge_2,
        *gathered,
    )
    beyond = lax.ppermute(beyond, both, end_pairs(slabs, blocks))
    state, source, mid_1 = call(
        functools.partial(place_edges, *sizes),
        [state_shape, source_shape, mid_shapes[0]],
        state,
        source,
        edge_1,
        edge_2,
        band,
        ghost,
        scratch=flux_scratch,
        aliases={0: 0, 1: 1},
        limit=12,
    )
    state, source, out = call(
        functools.partial(place_halos, *sizes[:3]),
        [state_shape, source_shape, (corner_layout(variables, cells)[1], lanes)],
        state,
        source,
        first,
        second,
        ghost,
        aliases={0: 0, 1: 1},
    )
    got = lax.ppermute(out, "blk", swap_pairs(blocks, 0))
    half_faces = (slabs // 2,) + face
    state, source, mid_1, mid_2, new, held, send = call(
        functools.partial(start_sections, *sizes),
        [state_shape, source_shape]
        + mid_shapes
        + [flow_state.shape, half_faces, half_faces],
        state,
        source,
        got,
        corner_1,
        corner_2,
        beyond,
        band,
        mid_1,
        scratch=flux_scratch,
        aliases={0: 0, 1: 1, 7: 2},
        limit=12,
    )
    step = slabs.bit_length() - 2
    spread = []
    if step > 0:
        low = [(i, i + (1 << step)) for i in range(0, slabs, 2 << step)]
        pairs = low + [(slabs - 1 - i, slabs - 1 - j) for i, j in low]
        spread.append(lax.ppermute(send, "pitch", pairs))
    _, _, new = call(
        functools.partial(finish_sections, *sizes),
        mid_shapes + [flow_state.shape],
        state,
        source,
        band,
        mid_1,
        mid_2,
        new,
        scratch=flux_scratch,
        aliases={3: 0, 4: 1, 5: 2},
        limit=12,
    )
    while step > 0:
        half_faces = (held.shape[0] // 2,) + face
        held, send = call(
            functools.partial(pass_on, step), [half_faces, half_faces], held, spread[-1], new
        )
        step -= 1
        if step > 0:
            low = [(i, i + (1 << step)) for i in range(0, slabs, 2 << step)]
            pairs = low + [(slabs - 1 - i, slabs - 1 - j) for i, j in low]
            spread.append(lax.ppermute(send, "pitch", pairs))
    second_sample = lax.ppermute(send, "pitch", flip_pairs(slabs, 1))
    parts = 4
    pieces = [orders * i // parts for i in range(parts + 1)]
    half_store = pltpu.VMEM(store.shape[1:], F32)
    new_state, new_store = call(
        functools.partial(close_first, pieces),
        [flow_state.shape, store.shape],
        new,
        store,
        table,
        held,
        scratch=[half_store, pltpu.SemaphoreType.DMA((parts + 1,))],
        out_specs=[HBM, HBM],
    )
    new_store, new_ghosts = call(
        functools.partial(close_second, pieces),
        [store.shape, (2,) + face],
        new_store,
        store,
        table,
        base,
        gain,
        held,
        second_sample,
        scratch=[half_store, pltpu.VMEM((2,) + face, F32), pltpu.SemaphoreType.DMA((parts + 1,))],
        in_specs=[HBM] + [VMEM] * 6,
        out_specs=[HBM, HBM],
        aliases={0: 0},
    )
    return (
        new_state,
        new_store.reshape(fourier_store.shape),
        new_ghosts.reshape(2, signals, part, lanes),
    )


def solution(mesh):
    placed = (
        P(None, "pitch", "blk", None),
        P(None, "pitch", "blk", None),
        P(None, None, None, ("blk", "pitch"), None),
        P(None, ("blk", "pitch"), None),
        P(("blk", "pitch"), None),
    )
    return jax.shard_map(
        shards,
        mesh=mesh,
        in_specs=placed,
        out_specs=(
            P(None, "pitch", "blk", None),
            P(None, None, None, ("blk", "pitch"), None),
            P(None, None, ("blk", "pitch"), None),
        ),
        check_vma=False,
    )
```

```python
import functools
import math

import jax
import jax.numpy as jnp
from jax import lax
from jax.experimental import pallas as pl
from jax.experimental.pallas import tpu as pltpu
from jax.sharding import PartitionSpec as P


NT = 96

gamma_less = 0.4
diss_coeff = 0.03125
section_coefs = (1.0 / 3.0, 0.5, 1.0)
pseudo_step = 0.1
physical_step = 0.25
relax_rate = 0.125
lag_turns = 0.3
period = 2.0 * math.pi / NT
phase_lag = 2.0 * math.pi * lag_turns

HF = 2 * len(section_coefs)
HP = HF - 2
PAD = 8

F32 = jnp.float32
VMEM = pl.BlockSpec(memory_space=pltpu.VMEM)


HBM = pl.BlockSpec(memory_space=pltpu.MemorySpace.HBM)


def call(body, outs, *args, scratch=(), aliases=None, in_specs=None, out_specs=None, types=None, cost=0, limit=8):
    outs = [jax.ShapeDtypeStruct(shape, kind) for shape, kind in zip(outs, types or [F32] * len(outs))]
    moved = 4 * sum(math.prod(a.shape) for a in list(args) + outs)
    return pl.pallas_call(
        body,
        out_shape=outs,
        in_specs=in_specs or [VMEM] * len(args),
        out_specs=out_specs or [VMEM] * len(outs),
        scratch_shapes=list(scratch),
        input_output_aliases=aliases or {},
        compiler_params=pltpu.CompilerParams(vmem_limit_bytes=limit << 20),
        cost_estimate=pl.CostEstimate(flops=cost, bytes_accessed=moved, transcendentals=0),
    )(*args)


def is_even(axis):
    return lax.axis_index(axis) % 2 == 0


def source_of(flow, prior):
    return (2.0 / physical_step) * flow - (0.5 / physical_step) * prior


def pack_pitch(cells, rows, state_ref, prior_ref, source_ref, first_ref, second_ref):
    own_rows = slice(PAD, PAD + rows)
    even = is_even("pitch")
    source_ref[:, HP : HP + cells, own_rows] = source_of(
        state_ref[:, HF : HF + cells, own_rows], prior_ref[...]
    )
    for out_ref, top in ((first_ref, even), (second_ref, jnp.logical_not(even))):
        at = jnp.where(top, cells, HF)
        out_ref[:, :HF] = state_ref[:, pl.ds(at, HF), own_rows]
        at = jnp.where(top, cells, HP)
        out_ref[:, HF:] = source_ref[:, pl.ds(at, HP), own_rows]


def pack_axial(cells, rows, state_ref, source_ref, edge_1, edge_2, corner_1, corner_2):
    refs = (state_ref, source_ref)
    edges, _ = edge_layout(state_ref.shape[0], cells, 0)
    sides, _ = side_layout(state_ref.shape[0])
    even = is_even("pitch")

    def write(up):
        for corner_ref, top in ((corner_1, even), (corner_2, jnp.logical_not(even))):
            for v, which, depth, count, place in sides:
                width = (HF, HP)[which]
                plane = jnp.where(top, width + cells - depth, width + depth - 1)
                corner_ref[place : place + count] = refs[which][v, plane, edge_rows(rows, count, up)]
        for v, which, plane, count, place in edges:
            edge_1[place : place + count] = refs[which][v, plane, edge_rows(rows, count, not up)]
            edge_2[place : place + count] = refs[which][v, plane, edge_rows(rows, count, up)]

    pl.when(is_even("blk"))(lambda: write(False))
    pl.when(jnp.logical_not(is_even("blk")))(lambda: write(True))


def edge_rows(rows, count, up):
    return slice(PAD + rows - count, PAD + rows) if up else slice(PAD, PAD + count)


def halo_rows(rows, count, up):
    return slice(PAD + rows, PAD + rows + count) if up else slice(PAD - count, PAD)


def doubled(values):
    return jnp.concatenate([values, values], axis=0)


def share_sent(step):
    return jnp.where(lax.axis_index("pitch") % (2 << step) == 1 << step, 0, 1)


def rebuild_shares(*refs):
    store_hbm, times_hbm, active_hbm, flow_hbm, prior_hbm = refs[:5]
    store_ref, times_ref, active_ref, state_ref, prior_ref, share_ref, send_ref = refs[5:12]
    band_ref, sems = refs[12:]
    cells, rows = flow_hbm.shape[1:3]
    copies = [
        pltpu.make_async_copy(from_ref, to_ref, sems.at[i])
        for i, (from_ref, to_ref) in enumerate(
            (
                (times_hbm, times_ref),
                (active_hbm, active_ref),
                (store_hbm.at[0], store_ref.at[0]),
                (store_hbm.at[1], store_ref.at[1]),
                (flow_hbm, state_ref.at[:, pl.ds(HF, cells), pl.ds(PAD, rows)]),
                (prior_hbm, prior_ref),
            )
        )
    ]
    for copy in copies:
        copy.start()
    band_ref[...] = radial_band(band_ref.shape[1]).astype(band_ref.dtype)
    copies[0].wait()
    copies[1].wait()
    harm_count = (store_ref.shape[1] - 1) // 2
    signals = store_ref.shape[2]
    active = doubled(active_ref[...])
    for which in range(2):
        angle = doubled(times_ref[which]).astype(F32) * period
        angle = angle - phase_lag if which == 0 else angle + phase_lag
        cos_1, sin_1 = jnp.cos(angle), jnp.sin(angle)
        copies[2 + which].wait()
        cos_k, sin_k = cos_1, sin_1
        totals = [store_ref[which, 0, v] for v in range(signals)]
        for k in range(1, harm_count + 1):
            used = active >= k
            a, b = jnp.where(used, cos_k, 0.0), jnp.where(used, sin_k, 0.0)
            for v in range(signals):
                totals[v] = totals[v] + (
                    store_ref[which, k, v] * a + store_ref[which, harm_count + k, v] * b
                )
            cos_k, sin_k = cos_k * cos_1 - sin_k * sin_1, sin_k * cos_1 + cos_k * sin_1
        for v in range(signals):
            share_ref[which, v] = totals[v]
    send_ref[0] = share_ref[share_sent(0)]
    copies[4].wait()
    copies[5].wait()


def join_shares(step, share_ref, *refs):
    got_refs, out_ref = refs[:-1], refs[-1]
    out_ref[0] = share_ref[share_sent(step)]
    at = 1
    for got_ref in got_refs:
        out_ref[at : at + got_ref.shape[0]] = got_ref[...]
        at += got_ref.shape[0]


def radial_band(lanes):
    shape = (2 * lanes, lanes)
    source = lax.broadcasted_iota(jnp.int32, shape, 0)
    target = lax.broadcasted_iota(jnp.int32, shape, 1)
    fluxes = source >= lanes
    source = jnp.where(fluxes, source - lanes, source)

    def at(ahead):
        return source == jnp.clip(target + ahead, 0, lanes - 1)

    def entries(pairs):
        total = jnp.zeros(shape, F32)
        for ahead, value in pairs:
            total = total + jnp.where(at(ahead), value, 0.0)
        return total

    own = 1.5 / physical_step - 18.0 * diss_coeff
    state = [(1, 4.0), (-1, 4.0), (2, -1.0), (-2, -1.0), (0, own / diss_coeff)]
    state = entries([(ahead, diss_coeff * value) for ahead, value in state])
    return jnp.where(fluxes, entries([(1, 1.0), (-1, -1.0)]), state)


def prepare_close(store_ref, times_ref, active_ref, after_ref, table_ref, base_ref, gain_ref):
    del after_ref
    harm_count = (store_ref.shape[1] - 1) // 2
    signals = store_ref.shape[2]
    active = doubled(active_ref[...])
    gain = jnp.full(active.shape, relax_rate, F32)
    for k in range(1, harm_count + 1):
        gain = gain + jnp.where(active >= k, 2.0 * relax_rate * math.cos(k * phase_lag), 0.0)
    gain_ref[...] = gain
    keep = 1.0 - relax_rate
    for which in range(2):
        angle = doubled(times_ref[which]).astype(F32) * period + period
        cos_1, sin_1 = jnp.cos(angle), jnp.sin(angle)
        cos_k, sin_k = cos_1, sin_1
        totals = [store_ref[which, 0, v] for v in range(signals)]
        turn = -phase_lag if which == 0 else phase_lag
        for k in range(1, harm_count + 1):
            table_ref[which, k - 1] = (2.0 * relax_rate) * cos_k
            table_ref[which, harm_count + k - 1] = (2.0 * relax_rate) * sin_k
            used = active >= k
            c, s = math.cos(k * turn), math.sin(k * turn)
            a = jnp.where(used, cos_k * c - sin_k * s, 0.0)
            b = jnp.where(used, sin_k * c + cos_k * s, 0.0)
            for v in range(signals):
                totals[v] = totals[v] + (
                    store_ref[which, k, v] * a + store_ref[which, harm_count + k, v] * b
                )
            cos_k, sin_k = cos_k * cos_1 - sin_k * sin_1, sin_k * cos_1 + cos_k * sin_1
        for v in range(signals):
            base_ref[which, v] = keep * totals[v]


def edge_layout(variables, cells, reach):
    parts, place = [], 0
    for v in range(variables):
        for which, width in ((0, HF), (1, HP)):
            out = min(reach, width - 1)
            for plane in range(-out, cells + out):
                count = width - max(0, -plane, plane - cells + 1)
                parts.append((v, which, plane + width, count, place))
                place += count
    return parts, -(-place // 8) * 8


def corner_layout(variables, cells):
    parts, place = [], 0
    for v, which, plane, count, _ in edge_layout(variables, cells, HF)[0]:
        if not 0 <= plane - (HF, HP)[which] < cells:
            parts.append((v, which, plane, count, place))
            place += count
    return parts, -(-place // 8) * 8


def side_layout(variables):
    parts, place = [], 0
    for v in range(variables):
        for which, width in ((0, HF), (1, HP)):
            for depth in range(1, width):
                parts.append((v, which, depth, width - depth, place))
                place += width - depth
    return parts, -(-place // 8) * 8


def halo_plane(cells, which, depth, upper):
    width = (HF, HP)[which]
    return jnp.where(upper, width + cells + depth - 1, width - depth)


def place_edges(cells, rows, slabs, blocks, *refs):
    edge_1, edge_2, band_ref = refs[2:5]
    state_ref, source_ref, mid_1 = refs[6:9]
    into = (state_ref, source_ref)
    edges, _ = edge_layout(state_ref.shape[0], cells, 0)

    def move(up):
        for v, which, plane, count, place in edges:
            into[which][v, plane, halo_rows(rows, count, not up)] = edge_1[place : place + count]
            into[which][v, plane, halo_rows(rows, count, up)] = edge_2[place : place + count]

    pl.when(is_even("blk"))(lambda: move(False))
    pl.when(jnp.logical_not(is_even("blk")))(lambda: move(True))
    block = Block(cells, rows, slabs, blocks, state_ref, source_ref, band_ref, refs[9:])
    block.clamp_ends(state_ref)
    block.advance(0, state_ref, mid_1, 2, cells - 2)


def join_ghosts(rows, slabs, share_ref, after_ref, *refs):
    del after_ref
    got_refs, (ghost_ref, send_ref) = refs[:-2], refs[-2:]
    part = rows // slabs
    variables = ghost_ref.shape[0]
    for end in range(2):

        @pl.when(lax.axis_index("pitch") == end * (slabs - 1))
        def _():
            pieces = [share_ref[end]]
            for got_ref in got_refs:
                pieces += [got_ref[i] for i in range(got_ref.shape[0])]
            for distance, piece in enumerate(pieces):
                at = part * (distance if end == 0 else slabs - 1 - distance)
                for layer in range(2):
                    ghost_ref[:, layer, at : at + part] = piece[:, layer * part : (layer + 1) * part]

    def write(at):
        for v in range(variables):
            for layer in range(2):
                place = (2 * v + layer) * HP
                send_ref[place : place + HP] = ghost_ref[v, layer, at : at + HP]

    pl.when(is_even("blk"))(lambda: write(0))
    pl.when(jnp.logical_not(is_even("blk")))(lambda: write(rows - HP))


def ghost_planes(cells, end):
    return HF + cells if end else HF - 2


def place_halos(cells, rows, slabs, *refs):
    first_ref, second_ref, ghost_ref = refs[2:5]
    state_ref, source_ref, out_ref = refs[-3:]
    refs = (state_ref, source_ref)
    even = is_even("pitch")
    variables = state_ref.shape[0]
    own_rows = slice(PAD, PAD + rows)
    for halo_ref, upper in ((first_ref, even), (second_ref, jnp.logical_not(even))):
        at = jnp.where(upper, HF + cells, 0)
        state_ref[:, pl.ds(at, HF), own_rows] = halo_ref[:, :HF]
        at = jnp.where(upper, HP + cells, 0)
        source_ref[:, pl.ds(at, HP), own_rows] = halo_ref[:, HF:]
    for end in range(2):

        @pl.when(lax.axis_index("pitch") == end * (slabs - 1))
        def _():
            plane = ghost_planes(cells, end)
            state_ref[:, plane : plane + 2, own_rows] = ghost_ref[...]

    corners, _ = corner_layout(variables, cells)

    def move(up):
        for v, which, plane, count, place in corners:
            out_ref[place : place + count] = refs[which][v, plane, edge_rows(rows, count, up)]

    pl.when(is_even("blk"))(lambda: move(True))
    pl.when(jnp.logical_not(is_even("blk")))(lambda: move(False))


class Block:
    def __init__(self, cells, rows, slabs, blocks, state_ref, source_ref, band_ref, flux_refs):
        self.cells, self.rows, self.slabs, self.blocks = cells, rows, slabs, blocks
        self.state_ref, self.source_ref, self.flux_refs = state_ref, source_ref, flux_refs
        self.band_ref = band_ref
        self.variables, _, _, self.lanes = state_ref.shape
        self.pitch_at = lax.axis_index("pitch")
        self.blk_at = lax.axis_index("blk")

    def clamp_ends(self, ref):
        rows = self.rows
        shape = (self.variables, ref.shape[1], 2, self.lanes)

        @pl.when(self.blk_at == 0)
        def _():
            ref[:, :, PAD - 2 : PAD] = jnp.broadcast_to(ref[:, :, PAD : PAD + 1], shape)

        @pl.when(self.blk_at == self.blocks - 1)
        def _():
            ref[:, :, PAD + rows : PAD + rows + 2] = jnp.broadcast_to(
                ref[:, :, PAD + rows - 1 : PAD + rows], shape
            )

    def keep_ghosts(self, ref, width):
        for end, at in ((0, 0), (self.slabs - 1, 2 + self.cells)):

            @pl.when(self.pitch_at == end)
            def _():
                ref[:, width - 2 + at : width + at] = self.state_ref[:, HF - 2 + at : HF + at]

    def advance(self, step, from_ref, to_ref, lo, hi):
        width = HF - 2 * step
        out_width = width - 2
        last = step == len(section_coefs) - 1
        scale = section_coefs[step] * pseudo_step
        count = -(-(self.rows + 2 * out_width) // 8) * 8
        row_at = PAD - out_width
        variables, lanes = self.variables, self.lanes
        pitch_ref, axial_ref, radial_ref = self.flux_refs

        flux_count = -(-(self.rows + 2 * out_width + 2) // 8) * 8
        flux_rows = slice(row_at - 1, row_at - 1 + flux_count)
        if flux_rows.stop > from_ref.shape[2]:
            flux_rows = slice(0, from_ref.shape[2])

        def fluxes(plane):
            u = [from_ref[v, plane + width, flux_rows] for v in range(variables)]
            inverse = 1.0 / u[0]
            speed = [u[d] * inverse for d in (1, 2, 3)]
            pressure = gamma_less * (
                u[4] - 0.5 * (u[1] * speed[0] + u[2] * speed[1] + u[3] * speed[2])
            )
            half = 0.5 * pressure
            total = u[4] + pressure
            for d, flux_ref in enumerate((pitch_ref, axial_ref, radial_ref)):
                w = 0.5 * speed[d]
                for v in (1, 2, 3):
                    flux = u[v] * w
                    flux_ref[v - 1, plane + HP + 1, flux_rows] = flux + half if v == d + 1 else flux
                flux_ref[3, plane + HP + 1, flux_rows] = total * w

        def update(plane):
            at = slice(row_at, row_at + count)
            here = [from_ref[v, plane + width, at] for v in range(variables)]
            along = [0.5 * here[3]] + [radial_ref[v, plane + HP + 1, at] for v in range(variables - 1)]
            values = jnp.concatenate(
                [jnp.concatenate(pair, axis=1) for pair in zip(here, along)], axis=0
            )
            coarse = values.astype(jnp.bfloat16)
            fine = (values - coarse.astype(F32)).astype(jnp.bfloat16)
            band = self.band_ref[...]
            radial = jnp.dot(coarse, band, preferred_element_type=F32) + jnp.dot(
                fine, band, preferred_element_type=F32
            )
            for v in range(variables):

                def state(ahead, over):
                    return from_ref[v, plane + width + ahead, row_at + over : row_at + over + count]

                def change_of(ref, d, ahead, over):
                    def flux(sign):
                        at = row_at + sign * over
                        at = slice(at, at + count)
                        if v == 0:
                            return from_ref[d, plane + width + sign * ahead, at]
                        return ref[v - 1, plane + HP + 1 + sign * ahead, at]

                    return flux(1) - flux(-1)

                change = change_of(pitch_ref, 1, 1, 0) + change_of(axial_ref, 2, 0, 1)
                if v == 0:
                    change = 0.5 * change
                near = (state(1, 0) + state(-1, 0)) + (state(0, 1) + state(0, -1))
                far = (state(2, 0) + state(-2, 0)) + (state(0, 2) + state(0, -2))
                change = change + ((4.0 * diss_coeff) * near - diss_coeff * far)
                change = change + radial[v * count : (v + 1) * count]
                source = self.source_ref[v, plane + HP, at]
                flow = self.state_ref[v, plane + HF, at]
                to_at = row_at - PAD if last else row_at
                to_ref[v, plane + out_width, to_at : to_at + count] = flow + scale * (source - change)

        def pairs(body, start, stop):
            def both(index, carry):
                plane = start + 2 * index
                body(plane)
                body(plane + 1)
                return carry

            lax.fori_loop(0, (stop - start) // 2, both, 0)

        pairs(fluxes, lo - 1, hi + 1)
        pairs(update, lo, hi)
        if not last:
            self.clamp_ends(to_ref)


def start_sections(cells, rows, slabs, blocks, *refs):
    got_ref, corner_1, corner_2, beyond_ref, band_ref = refs[2:7]
    state_ref, source_ref, mid_1, mid_2, new_ref, kept_ref, sent_ref = refs[8:15]
    flux_refs = refs[15:]
    block = Block(cells, rows, slabs, blocks, state_ref, source_ref, band_ref, flux_refs)
    variables = state_ref.shape[0]
    even = is_even("pitch")
    sides, _ = side_layout(variables)
    corners, _ = corner_layout(variables, cells)
    into = (state_ref, source_ref)

    def unpack(up):
        for v, which, plane, count, place in corners:
            into[which][v, plane, halo_rows(rows, count, not up)] = got_ref[place : place + count]
        for corner_ref, upper in ((corner_1, even), (corner_2, jnp.logical_not(even))):
            for v, which, depth, count, place in sides:
                plane = halo_plane(cells, which, depth, upper)
                into[which][v, plane, halo_rows(rows, count, up)] = corner_ref[place : place + count]
        for end in range(2):

            @pl.when(block.pitch_at == end * (slabs - 1))
            def _():
                for v in range(variables):
                    for layer in range(2):
                        place = (2 * v + layer) * HP
                        plane = ghost_planes(cells, end) + layer
                        state_ref[v, plane, halo_rows(rows, HP, up)] = beyond_ref[place : place + HP]

    pl.when(is_even("blk"))(lambda: unpack(False))
    pl.when(jnp.logical_not(is_even("blk")))(lambda: unpack(True))
    block.clamp_ends(state_ref)
    block.keep_ghosts(mid_1, HF - 2)
    block.keep_ghosts(mid_2, HF - 4)
    part = rows // slabs
    high = block.pitch_at == slabs - 1

    @pl.when((block.pitch_at == 0) | high)
    def _():
        for step, (from_ref, to_ref) in enumerate(
            ((state_ref, mid_1), (mid_1, mid_2), (mid_2, new_ref))
        ):
            planes = 2 if step == 0 else HF - 2 * step
            lo = jnp.where(high, cells - planes, 0)
            block.advance(step, from_ref, to_ref, lo, lo + planes)

    for end, plane in ((0, 0), (slabs - 1, cells - 2)):

        @pl.when(block.pitch_at == end)
        def _():
            for j in range(slabs):
                out_ref, i = (kept_ref, j) if 2 * j < slabs else (sent_ref, j - slabs // 2)
                at = (end ^ j) * part
                for layer in range(2):
                    out_ref[i, :, layer * part : (layer + 1) * part] = new_ref[
                        :, plane + layer, at : at + part
                    ]


def finish_sections(cells, rows, slabs, blocks, *refs):
    state_ref, source_ref, band_ref = refs[:3]
    mid_1, mid_2, new_ref = refs[6:9]
    block = Block(cells, rows, slabs, blocks, state_ref, source_ref, band_ref, refs[9:])
    low, high = block.pitch_at == 0, block.pitch_at == slabs - 1
    width = HF - 2
    pl.when(jnp.logical_not(low))(lambda: block.advance(0, state_ref, mid_1, -width, 2))
    pl.when(jnp.logical_not(high))(
        lambda: block.advance(0, state_ref, mid_1, cells - 2, cells + width)
    )
    for step, from_ref, to_ref in ((1, mid_1, mid_2), (2, mid_2, new_ref)):
        done = HF - 2 * step
        out_width = done - 2
        lo = jnp.where(low, done, -out_width)
        hi = jnp.where(high, cells - done, cells + out_width)
        block.advance(step, from_ref, to_ref, lo, hi)


def pass_on(step, held_ref, got_ref, after_ref, kept_ref, sent_ref):
    del after_ref
    at = lax.axis_index("pitch") % (2 << step)
    half = kept_ref.shape[0]
    got = (at == 1 << step) | (at == (1 << step) - 1)

    @pl.when(got)
    def _():
        kept_ref[...] = got_ref[:half]
        sent_ref[...] = got_ref[half:]

    @pl.when(jnp.logical_not(got))
    def _():
        kept_ref[...] = held_ref[:half]
        sent_ref[...] = held_ref[half:]


def refresh_half(pieces, which, sample_ref, store_ref, table_ref, fresh_ref, out_ref, send):
    keep = 1.0 - relax_rate
    sample = [sample_ref[0, v] for v in range(store_ref.shape[2])]
    for lo, hi in zip(pieces[:-1], pieces[1:]):
        for k in range(lo, hi):
            weight = relax_rate if k == 0 else table_ref[which, k - 1]
            for v, value in enumerate(sample):
                fresh_ref[k, v] = keep * store_ref[which, k, v] + weight * value
        window = pl.ds(lo, hi - lo)
        send(fresh_ref.at[window], out_ref.at[which, window])


def sender(sems):
    copies = []

    def send(from_ref, to_ref):
        copy = pltpu.make_async_copy(from_ref, to_ref, sems.at[len(copies)])
        copy.start()
        copies.append(copy)

    return copies, send


def close_first(pieces, new_ref, store_ref, table_ref, sample_ref, state_hbm, out_ref, fresh_ref, sems):
    copies, send = sender(sems)
    send(new_ref, state_hbm)
    which = 1 - lax.axis_index("pitch") % 2
    refresh_half(pieces, which, sample_ref, store_ref, table_ref, fresh_ref, out_ref, send)
    for copy in copies:
        copy.wait()


def close_second(pieces, *refs):
    store_ref, table_ref, base_ref, gain_ref, first_ref, second_ref = refs[1:7]
    out_ref, ghost_hbm, fresh_ref, ghost_ref, sems = refs[7:]
    copies, send = sender(sems)
    which = lax.axis_index("pitch") % 2
    gain = gain_ref[...]
    for at, sample_ref in ((1 - which, first_ref), (which, second_ref)):
        ghost_ref[at] = base_ref[at] + sample_ref[0] * gain[None]
    send(ghost_ref, ghost_hbm)
    refresh_half(pieces, which, second_ref, store_ref, table_ref, fresh_ref, out_ref, send)
    for copy in copies:
        copy.wait()


def swap_pairs(count, start):
    pairs = [(i, i + 1) for i in range(start, count - 1, 2)]
    return pairs + [(b, a) for a, b in pairs]


def flip_pairs(count, bits):
    return [(i, i ^ bits) for i in range(count)]


def diagonal_pairs(slabs, blocks, start):
    return [
        (b * slabs + p, other * slabs + q)
        for b, other in swap_pairs(blocks, 1)
        for p, q in swap_pairs(slabs, start)
    ]


def end_pairs(slabs, blocks):
    return [
        (b * slabs + p, other * slabs + p)
        for b, other in swap_pairs(blocks, 1)
        for p in (0, slabs - 1)
    ]


def shards(flow_state, prior_state, fourier_store, sample_times, harmonics):
    slabs = lax.axis_size("pitch")
    blocks = lax.axis_size("blk")
    variables, cells, rows, lanes = flow_state.shape
    orders, signals, part = fourier_store.shape[1:4]
    store = fourier_store.reshape(2, orders, variables, 2 * part, lanes)
    halo = (variables, HF + HP, rows, lanes)
    face = (variables, 2 * part, lanes)
    long_rows = rows + 2 * PAD
    state_shape = (variables, cells + 2 * HF, long_rows, lanes)
    source_shape = (variables, cells + 2 * HP, long_rows, lanes)

    inputs = (store, sample_times, harmonics, flow_state, prior_state)
    shapes = [store.shape, sample_times.shape, harmonics.shape, state_shape, flow_state.shape]
    store, times, active, state, prior, share, send, band = call(
        rebuild_shares,
        shapes + [(2,) + face, (1,) + face, (2 * lanes, lanes)],
        *[pltpu.with_memory_space_constraint(a, pltpu.MemorySpace.HBM) for a in inputs],
        types=(F32, jnp.int32, jnp.int32, F32, F32, F32, F32, jnp.bfloat16),
        scratch=[pltpu.SemaphoreType.DMA((len(inputs) + 1,))],
        in_specs=[HBM] * len(inputs),
    )
    gathered, step = [lax.ppermute(send, "pitch", flip_pairs(slabs, 1))], 1
    source, first, second = call(
        functools.partial(pack_pitch, cells, rows), [source_shape, halo, halo], state, prior
    )
    first = lax.ppermute(first, "pitch", swap_pairs(slabs, 0))
    second = lax.ppermute(second, "pitch", swap_pairs(slabs, 1))
    edge_shape = (edge_layout(variables, cells, 0)[1], lanes)
    side_shape = (side_layout(variables)[1], lanes)
    edge_1, edge_2, corner_1, corner_2 = call(
        functools.partial(pack_axial, cells, rows),
        [edge_shape, edge_shape, side_shape, side_shape],
        state,
        source,
    )
    edge_2 = lax.ppermute(edge_2, "blk", swap_pairs(blocks, 1))
    edge_1 = lax.ppermute(edge_1, "blk", swap_pairs(blocks, 0))
    both = ("blk", "pitch")
    corner_1 = lax.ppermute(corner_1, both, diagonal_pairs(slabs, blocks, 0))
    corner_2 = lax.ppermute(corner_2, both, diagonal_pairs(slabs, blocks, 1))
    while 1 << step < slabs:
        [send] = call(
            functools.partial(join_shares, step), [(1 << step,) + face], share, *gathered
        )
        gathered.append(lax.ppermute(send, "pitch", flip_pairs(slabs, 1 << step)))
        step += 1
    sizes = (cells, rows, slabs, blocks)
    mid_shapes = [
        (variables, cells + 2 * HP, long_rows, lanes),
        (variables, cells + 2 * HP - 4, long_rows, lanes),
    ]
    flux_shape = (variables - 1, cells + 2 * HP + 2, long_rows, lanes)
    flux_scratch = [pltpu.VMEM(flux_shape, F32)] * 3
    ghost, beyond = call(
        functools.partial(join_ghosts, rows, slabs),
        [(variables, 2, rows, lanes), (2 * variables * HP, lanes)],
        share,
        edge_2,
        *gathered,
    )
    beyond = lax.ppermute(beyond, both, end_pairs(slabs, blocks))
    state, source, mid_1 = call(
        functools.partial(place_edges, *sizes),
        [state_shape, source_shape, mid_shapes[0]],
        state,
        source,
        edge_1,
        edge_2,
        band,
        ghost,
        scratch=flux_scratch,
        aliases={0: 0, 1: 1},
        limit=12,
    )
    state, source, out = call(
        functools.partial(place_halos, *sizes[:3]),
        [state_shape, source_shape, (corner_layout(variables, cells)[1], lanes)],
        state,
        source,
        first,
        second,
        ghost,
        aliases={0: 0, 1: 1},
    )
    got = lax.ppermute(out, "blk", swap_pairs(blocks, 0))
    half_faces = (slabs // 2,) + face
    state, source, mid_1, mid_2, new, held, send = call(
        functools.partial(start_sections, *sizes),
        [state_shape, source_shape]
        + mid_shapes
        + [flow_state.shape, half_faces, half_faces],
        state,
        source,
        got,
        corner_1,
        corner_2,
        beyond,
        band,
        mid_1,
        scratch=flux_scratch,
        aliases={0: 0, 1: 1, 7: 2},
        limit=12,
    )
    step = slabs.bit_length() - 2
    spread = []
    if step > 0:
        low = [(i, i + (1 << step)) for i in range(0, slabs, 2 << step)]
        pairs = low + [(slabs - 1 - i, slabs - 1 - j) for i, j in low]
        spread.append(lax.ppermute(send, "pitch", pairs))
    _, _, new = call(
        functools.partial(finish_sections, *sizes),
        mid_shapes + [flow_state.shape],
        state,
        source,
        band,
        mid_1,
        mid_2,
        new,
        scratch=flux_scratch,
        aliases={3: 0, 4: 1, 5: 2},
        limit=12,
    )
    table, base, gain = call(
        prepare_close,
        [(2, orders - 1, 2 * part, lanes), (2,) + face, (2 * part, lanes)],
        store,
        times,
        active,
        new,
    )

    while step > 0:
        half_faces = (held.shape[0] // 2,) + face
        held, send = call(
            functools.partial(pass_on, step), [half_faces, half_faces], held, spread[-1], new
        )
        step -= 1
        if step > 0:
            low = [(i, i + (1 << step)) for i in range(0, slabs, 2 << step)]
            pairs = low + [(slabs - 1 - i, slabs - 1 - j) for i, j in low]
            spread.append(lax.ppermute(send, "pitch", pairs))
    second_sample = lax.ppermute(send, "pitch", flip_pairs(slabs, 1))
    parts = 2
    pieces = [orders * i // parts for i in range(parts + 1)]
    half_store = pltpu.VMEM(store.shape[1:], F32)
    new_state, new_store = call(
        functools.partial(close_first, pieces),
        [flow_state.shape, store.shape],
        new,
        store,
        table,
        held,
        scratch=[half_store, pltpu.SemaphoreType.DMA((parts + 1,))],
        out_specs=[HBM, HBM],
    )
    new_store, new_ghosts = call(
        functools.partial(close_second, pieces),
        [store.shape, (2,) + face],
        new_store,
        store,
        table,
        base,
        gain,
        held,
        second_sample,
        scratch=[half_store, pltpu.VMEM((2,) + face, F32), pltpu.SemaphoreType.DMA((parts + 1,))],
        in_specs=[HBM] + [VMEM] * 6,
        out_specs=[HBM, HBM],
        aliases={0: 0},
    )
    return (
        new_state,
        new_store.reshape(fourier_store.shape),
        new_ghosts.reshape(2, signals, part, lanes),
    )


def solution(mesh):
    placed = (
        P(None, "pitch", "blk", None),
        P(None, "pitch", "blk", None),
        P(None, None, None, ("blk", "pitch"), None),
        P(None, ("blk", "pitch"), None),
        P(("blk", "pitch"), None),
    )
    return jax.shard_map(
        shards,
        mesh=mesh,
        in_specs=placed,
        out_specs=(
            P(None, "pitch", "blk", None),
            P(None, None, None, ("blk", "pitch"), None),
            P(None, None, ("blk", "pitch"), None),
        ),
        check_vma=False,
    )
```
